32 devices in a mesh: grp: 2 (over y), seq: 4 (over z), head: 2 (over x), rep: 2 (over core).
Axes of the slice: x: 2, y: 2, z: 4, core: 2. Of those that a mesh axis runs over, the one named last changes fastest.
Arguments:
- tokens: bfloat16 [4096, 2048], P(('grp', 'seq'), 'rep'), parts along dimension 0, may hold values from -30 to 30, as said below
- projection: bfloat16 [2048, 3, 2048], P('rep', None, 'head'), may hold values from -0.116009706 to 0.116009706, as said below
- rand_table: int32 [16, 32, 3], P(('head', 'rep')), may hold values from 2 to 6
- round_masks: int32 [3], replicated, may hold values from 1 to 3, as said below
Outputs:
- context: bfloat16 [4096, 2048], P(('grp', 'seq'), ('head', 'rep')), parts along dimension 0
The draws below stay inside these ranges and needn't reach their ends.
There are 2 independent parts, one for each index of `grp`. The reference program is written for one: setup_inputs(seed, part) draws one part's arguments, and reference() takes and returns one part's arrays. A program takes and returns all parts, laid end to end along the dimension named above; an argument that names none is the same for every part. Nothing has to cross between parts.
Inputs may be any that keep to these rules, and one draw needn't show every extreme that they name: `tokens`: floats of the inputs; a few rows may be larger than the rest. `projection`: query and key columns are scaled a little above the fan-in rule. 3 distinct values; in round r shard i is paired with shard i xor round_masks[r]; one of them is 3. `rand_table`: an entry names a block inside the partner shard, never its first two nor its last.
All inputs are finite; a program needn't handle non-finite values.
Results may differ from the reference program's by a relative error of at most 0.0011.
The reference program's roundings to bfloat16 on the way count: a program that leaves them out, or rounds other values in their place, can miss the bound.
Values may be sent and summed in bfloat16 or wider, within the bound.
A program may use at most 128 MiB of HBM per device.

```python
import jax
import jax.numpy as jnp
from jax import lax

D = 2048
H = 16
HD = 128
B = 64
R = 3
SHARDS = 4
TOKENS = 2048
BPS = 8
NBLK = 32
HH = 2048


def draw_tokens(key, part):
    base = jnp.clip(jax.random.normal(key, (TOKENS, D), jnp.float32), -5.0, 5.0)
    result = base * 4.0
    return result.astype(jnp.bfloat16)


def draw_projection(key, part):
    first_key = jax.random.fold_in(key, 11)
    base = jnp.clip(jax.random.normal(first_key, (D, 3, HH), jnp.float32), -3.5, 3.5)
    factors = jnp.array([1.48, 1.48, 0.25], jnp.float32) / D ** 0.5
    result = base * factors[None, :, None]
    return result.astype(jnp.bfloat16)


def draw_round_masks(key, part):
    order_key = jax.random.fold_in(key, 5)
    place_key = jax.random.fold_in(key, 7)
    values = jax.random.permutation(order_key, SHARDS - 1) + 1
    top_place = jnp.argmax(values)
    chosen = values[:R]
    place = jax.random.randint(place_key, (), 0, R)
    chosen = jnp.where(top_place >= R, chosen.at[place].set(SHARDS - 1), chosen)
    return chosen.astype(jnp.int32)


def plant(values, rng, least, high):
    extent = values.shape
    spot = [jax.random.randint(jax.random.fold_in(rng, axis), (), 0, extent[axis]) for axis in range(len(extent))]
    values = values.at[tuple(spot)].set(least)
    longest = extent.index(max(extent))
    spot[longest] = (spot[longest] + 1) % extent[longest]
    return values.at[tuple(spot)].set(high)


def setup_inputs(seed: int = 0, part: int = 0) -> dict:
    keys = jax.random.split(jax.random.key(seed), 5)
    part_keys = jax.random.split(jax.random.fold_in(keys[4], part), 5)
    return {
        "tokens": draw_tokens(jax.random.fold_in(jax.random.fold_in(keys[4], part), 71), part),
        "projection": draw_projection(jax.random.fold_in(keys[4], 71), part),
        "rand_table": plant(jax.random.randint(keys[2], (H, NBLK, R), 2, BPS - 1), jax.random.fold_in(keys[2], 1), 2, (BPS - 1) - 1).astype(jnp.int32),
        "round_masks": draw_round_masks(jax.random.fold_in(keys[4], 71), part),
    }


def window_allowed():
    block_ids = jnp.arange(NBLK, dtype=jnp.int32)
    nearby = block_ids[:, None] - 1 + jnp.arange(3, dtype=jnp.int32)[None, :]
    allowed = (nearby >= 2) & (nearby < NBLK)
    allowed = jnp.repeat(allowed, B, axis=1)
    return jnp.concatenate([allowed, jnp.ones((NBLK, (2 + R) * B), dtype=bool)], axis=1)


def gather_keys(flat_rows, table_head, round_masks):
    blocked = flat_rows.reshape(NBLK, B, HD)
    zero_block = jnp.zeros((1, B, HD), flat_rows.dtype)
    padded = jnp.concatenate([zero_block, blocked, zero_block], axis=0)
    window_part = jnp.concatenate([padded[0:NBLK], padded[1:NBLK + 1], padded[2:NBLK + 2]], axis=1)
    global_part = jnp.broadcast_to(flat_rows[:2 * B][None], (NBLK, 2 * B, HD))
    block_ids = jnp.arange(NBLK, dtype=jnp.int32)
    partner = jnp.bitwise_xor((block_ids // BPS)[:, None], round_masks[None, :].astype(jnp.int32))
    source = (partner * BPS + table_head.astype(jnp.int32)).astype(jnp.int32)
    random_part = blocked[source].reshape(NBLK, R * B, HD)
    return jnp.concatenate([window_part, global_part, random_part], axis=1)


def reference(tokens, projection, rand_table, round_masks):
    scale = HD ** -0.5
    mixed_rows = jnp.dot(tokens, projection.reshape(D, 3 * H * HD), preferred_element_type=jnp.float32).astype(jnp.bfloat16)
    mixed_rows = mixed_rows.reshape(TOKENS, 3, H, HD).transpose(1, 2, 0, 3)
    allowed = window_allowed()

    def one_head(inputs):
        queries, key_rows, value_rows, table_head = inputs
        all_keys = gather_keys(key_rows, table_head, round_masks)
        all_values = gather_keys(value_rows, table_head, round_masks)
        blocked_queries = queries.reshape(NBLK, B, HD)
        scores = jnp.einsum('gqe,gke->gqk', blocked_queries.astype(jnp.float32), all_keys.astype(jnp.float32), precision=lax.Precision.HIGHEST) * scale
        scores = jnp.where(allowed[:, None, :], scores, -jnp.inf)
        peak = jnp.max(scores, axis=-1, keepdims=True)
        expd = jnp.exp(scores - peak)
        row_total = jnp.sum(expd, axis=-1, keepdims=True)
        weights = expd.astype(jnp.bfloat16)
        regular = jnp.einsum('gqk,gke->gqe', weights.astype(jnp.float32), all_values.astype(jnp.float32), precision=lax.Precision.HIGHEST) / row_total
        gscores = jnp.dot(queries[:2 * B].astype(jnp.float32), key_rows.astype(jnp.float32).T, precision=lax.Precision.HIGHEST) * scale
        gpeak = jnp.max(gscores, axis=-1, keepdims=True)
        gexp = jnp.exp(gscores - gpeak)
        gtotal = jnp.sum(gexp, axis=-1, keepdims=True)
        gacc = jnp.dot(gexp, value_rows.astype(jnp.float32), precision=lax.Precision.HIGHEST)
        rows_out = regular.reshape(TOKENS, HD)
        rows_out = rows_out.at[:2 * B].set(gacc / gtotal)
        return rows_out.astype(jnp.bfloat16)

    per_head = lax.map(one_head, (mixed_rows[0], mixed_rows[1], mixed_rows[2], rand_table))
    return per_head.transpose(1, 0, 2).reshape(TOKENS, H * HD)
```

```python
import functools

import jax
import jax.numpy as jnp
from jax import lax
from jax.experimental import pallas as pl
from jax.experimental.pallas import tpu as pltpu
from jax.sharding import PartitionSpec as P

HD = 128
B = 64
R = 3


def with_halo(block, sides, width):
    for axis, dim in sides:
        count = lax.axis_size(axis)
        forward = [(i, i + 1) for i in range(count - 1)]
        backward = [(target, source) for source, target in forward]
        low = lax.ppermute(
            lax.slice_in_dim(block, block.shape[dim] - width, None, axis=dim), axis, forward
        )
        high = lax.ppermute(lax.slice_in_dim(block, 0, width, axis=dim), axis, backward)
        block = jnp.concatenate([low, block, high], axis=dim)
    return block


def spread(shard, axis, root):
    mine = lax.axis_index(axis) == root
    return lax.psum(jnp.where(mine, shard, jnp.zeros_like(shard)), axis)


def from_partner(block, axis, apart):
    count = lax.axis_size(axis)
    route = []
    for low in range(count):
        high = low | 1 << apart
        if high != low and high < count:
            route += [(low, high), (high, low)]
    return lax.ppermute(block, axis, route)


def combined_all(part, axis, combine):
    gathered = jax.tree.map(lambda a: lax.all_gather(a, axis), part)

    def take(source):
        return jax.tree.map(lambda a: lax.dynamic_index_in_dim(a, source, 0, False), gathered)

    return lax.fori_loop(
        1, lax.axis_size(axis), lambda source, state: combine(state, take(source)), take(0)
    )


def combine_parts(former, latter):
    peak = jnp.maximum(former[0], latter[0])
    former_scale = jnp.exp(former[0] - peak)
    latter_scale = jnp.exp(latter[0] - peak)
    summed = former[1] * former_scale + latter[1] * latter_scale
    accum = former[2] * former_scale[..., None] + latter[2] * latter_scale[..., None]
    return (peak, summed, accum)


def take_blocks(source, indices):
    return jnp.take(source, indices, axis=1)


def bit_set(mask_value, bit_pos):
    return jnp.bitwise_and(jnp.right_shift(mask_value, bit_pos), 1) == 1


def body(tokens, projection, rand_table, round_masks):
    scale = HD ** (-0.5)
    tok_count = tokens.shape[0]
    width_local = tokens.shape[1]
    heads_group = projection.shape[2] // HD
    heads_here = heads_group // lax.axis_size("rep")
    blocks_here = tok_count // B
    shaped = projection.reshape(width_local, 3, heads_group, HD)
    summed = lax.psum_scatter(
        jnp.einsum("td,dshe->htse", tokens, shaped, preferred_element_type=jnp.float32),
        "rep",
        scatter_dimension=0,
        tiled=True,
    )
    mixed_rows = summed.astype(jnp.bfloat16)
    queries = mixed_rows[:, :, 0]
    key_vals = jnp.moveaxis(mixed_rows[:, :, 1:], 2, 0)
    shard_id = lax.axis_index("seq")
    shards = lax.axis_size("seq")
    total_blocks = shards * blocks_here
    padded = with_halo(key_vals, (("seq", 2),), B)
    window = jnp.stack(
        [
            padded[:, :, offset * B : offset * B + tok_count].reshape(
                2, heads_here, blocks_here, B, HD
            )
            for offset in range(3)
        ],
        axis=3,
    )
    window = window.reshape(2, heads_here, blocks_here, 3 * B, HD)
    lead_queries, lead_keys = (
        spread(queries[:, : 2 * B], "seq", 0),
        spread(key_vals[:, :, : 2 * B], "seq", 0),
    )
    global_part = jnp.broadcast_to(lead_keys[:, :, None], (2, heads_here, blocks_here, 2 * B, HD))
    blocked = key_vals.reshape(2, heads_here, blocks_here, B, HD)
    bit_count = shards.bit_length() - 1
    fetched = []
    for round_id in range(R):
        peer = jnp.bitwise_xor(shard_id, round_masks[round_id])
        wanted = lax.dynamic_slice_in_dim(
            rand_table[:, :, round_id], peer * blocks_here, blocks_here, 1
        )
        payload = jax.vmap(take_blocks, in_axes=(1, 0), out_axes=1)(blocked, wanted)
        for bit_pos in range(bit_count):
            swapped = from_partner(payload, "seq", bit_pos)
            payload = jnp.where(bit_set(round_masks[round_id], bit_pos), swapped, payload)
        fetched.append(payload)
    random_part = jnp.concatenate(fetched, axis=3)
    all_keys = jnp.concatenate([window, global_part, random_part], axis=3)
    block_ids = shard_id * blocks_here + jnp.arange(blocks_here, dtype=jnp.int32)
    nearby = block_ids[:, None] - 1 + jnp.arange(3, dtype=jnp.int32)[None, :]
    allowed = (nearby >= 2) & (nearby < total_blocks)
    allowed = jnp.repeat(allowed, B, axis=1)
    allowed = jnp.concatenate([allowed, jnp.ones((blocks_here, (2 + R) * B), dtype=bool)], axis=1)
    blocked_queries = queries.reshape(heads_here, blocks_here, B, HD)
    scores = (
        jnp.einsum(
            "hjqe,hjke->hjqk", blocked_queries, all_keys[0], preferred_element_type=jnp.float32
        )
        * scale
    )
    scores = jnp.where(allowed[None, :, None, :], scores, -jnp.inf)
    peak = jnp.max(scores, axis=-1, keepdims=True)
    expd = jnp.exp(scores - peak)
    row_total = jnp.sum(expd, axis=-1, keepdims=True)
    weights = expd.astype(jnp.bfloat16)
    regular = jnp.einsum(
        "hjqk,hjke->jqhe", weights, all_keys[1], preferred_element_type=jnp.float32
    )
    regular = regular / jnp.moveaxis(row_total, 0, 2)
    regular = regular.reshape(tok_count, heads_here, HD)
    gscores = (
        jnp.einsum("hqe,hke->hqk", lead_queries, key_vals[0], preferred_element_type=jnp.float32)
        * scale
    )
    local_peak = jnp.max(gscores, axis=-1)
    local_exp = jnp.exp(gscores - local_peak[..., None])
    local_sum = jnp.sum(local_exp, axis=-1)
    local_acc = jnp.einsum(
        "hqk,hke->hqe", local_exp, key_vals[1].astype(jnp.float32), precision=lax.Precision.HIGHEST
    )
    merged = combined_all((local_peak, local_sum, local_acc), "seq", combine_parts)
    global_rows = jnp.transpose(merged[2] / merged[1][..., None], (1, 0, 2))
    global_full = jnp.pad(global_rows, ((0, tok_count - 2 * B), (0, 0), (0, 0)))
    row_ids = jnp.arange(tok_count)
    use_global = (shard_id == 0) & (row_ids < 2 * B)
    combined = jnp.where(use_global[:, None, None], global_full, regular)
    return combined.reshape(tok_count, heads_here * HD).astype(jnp.bfloat16)


MESH = pl.DeviceIdType.MESH
DEPTH = 2 * B
OWNER = 1
X_LAG = 4
C_LAG = 6
M_LAG = 2
OWN_STEP = 5
CONTRACT = (((1,), (1,)), ((), ()))


def layer_kernel(
    shards, table_ref, mask_ref, tok_ref, w_ref, o_ref,
    full, wfull, q_s, k_s, v_s, g_q, g_max, g_sum, g_acc, g_out, g_in,
    zsend, zrecv, fsend, frecv, xsend, xrecv, csend, crecv, wsend, wrecv, lsem, gsem,
):
    s, x, c = lax.axis_index("seq"), lax.axis_index("head"), lax.axis_index("rep")
    rows, width = tok_ref.shape
    cols = width // 2
    mine = w_ref.shape[2] // 2
    heads = mine // HD
    blocks = rows // B
    total = shards * blocks
    steps = (shards - 1) * blocks
    scale = HD ** (-0.5)
    has_up, has_down = s < shards - 1, s > 0
    up, down = {"seq": s + 1}, {"seq": s - 1}
    across, core = {"head": 1 - x}, {"rep": 1 - c}
    rising = s >= shards // 2
    inner = has_up & has_down
    far = jnp.where(rising, shards - 1, 0)

    barrier = pltpu.get_barrier_semaphore()

    def greet(device):
        pl.semaphore_signal(barrier, inc=1, device_id=device, device_id_type=MESH)

    greet(across)
    greet(core)

    @pl.when(has_up)
    def _():
        greet(up)

    @pl.when(has_down)
    def _():
        greet(down)

    pl.semaphore_wait(barrier, 2 + has_up.astype(jnp.int32) + has_down.astype(jnp.int32))

    def remote(src, dst, send, recv, device):
        return pltpu.make_async_remote_copy(
            src_ref=src, dst_ref=dst, send_sem=send, recv_sem=recv, device_id=device, device_id_type=MESH
        )

    def rows_of(i, size=B):
        return pl.ds(pl.multiple_of(i * size, size), size)

    def quarter(i):
        return pl.ds(pl.multiple_of(c * width + i * cols, cols), cols)

    def half(i):
        return pl.ds(pl.multiple_of(i * width, width), width)

    def drawable(b):
        return (b >= 2) & (b < blocks - 1)

    def goes_up(at, src, b):
        return drawable(b) | ((b < 2) & (src == 0)) | ((b == blocks - 1) & (src == at))

    def goes_down(at, src, b):
        return drawable(b) | ((b == 0) & (src == at)) | (at > OWNER)

    def own_z(i, way):
        piece = tok_ref.at[rows_of(i), pl.ds(pl.multiple_of(x * cols, cols), cols)]
        return remote(piece, full.at[s, rows_of(i), quarter(x)], zsend.at[way, s, i], zrecv.at[s, i], (down, up)[way])

    def own_f(i, way):
        piece = tok_ref.at[rows_of(i), pl.ds(pl.multiple_of((1 - x) * cols, cols), cols)]
        return remote(piece, full.at[s, rows_of(i), quarter(1 - x)], fsend.at[i], frecv.at[i], (down, up)[way])

    def relay_z(src, i, way):
        piece = full.at[src, rows_of(i), quarter(x)]
        return remote(piece, piece, zsend.at[way, src, i], zrecv.at[src, i], (down, up)[way])

    def landed_f(i):
        piece = full.at[far, rows_of(i), quarter(1 - x)]
        return remote(piece, piece, fsend.at[i], frecv.at[i], down)

    def relay_x(src, i, which):
        piece = full.at[src, rows_of(i), quarter(which)]
        return remote(piece, piece, xsend.at[src, i], xrecv.at[src, i], across)

    def relay_c(src, i, which):
        piece = full.at[src, rows_of(i), half(which)]
        return remote(piece, piece, csend.at[src, i], crecv.at[src, i], core)

    def own_c(which):
        return remote(tok_ref, full.at[s, :, half(which)], wsend.at[3], wrecv.at[3], core)

    def weight_c(i, which):
        theirs = w_ref.at[i, :, pl.ds(pl.multiple_of((1 - c) * mine, mine), mine)]
        return remote(theirs, wfull.at[i, half(which), :], wsend.at[i], wrecv.at[i], core)

    def weight_l(i):
        own = w_ref.at[i, :, pl.ds(pl.multiple_of(c * mine, mine), mine)]
        return pltpu.make_async_copy(own, wfull.at[i, half(c), :], lsem.at[i])

    own_l = pltpu.make_async_copy(tok_ref, full.at[s, :, half(c)], lsem.at[3])

    def result():
        return remote(g_out, g_in, gsem.at[0], gsem.at[1], {"seq": OWNER - 1})

    def near(b):
        return drawable(b) | (b == 0) | (s < shards - 1)

    def own_sends(act):
        def one(i, carry):
            @pl.when(has_up & goes_up(s, s, i))
            def _():
                act(own_z(i, 1))

            @pl.when(has_down & goes_down(s, s, i))
            def _():
                act(own_z(i, 0))

            return carry

        lax.fori_loop(0, blocks, one, 0)

        def other(i, carry):
            @pl.when(s == 0)
            def _():
                act(own_f(i, 1))

            @pl.when((s == shards - 1) & (drawable(i) | (i == 0)))
            def _():
                act(own_f(i, 0))

            return carry

        lax.fori_loop(0, blocks, other, 0)

    own_sends(lambda copy: copy.start())
    own_l.start()
    own_c(c).start()
    for i in (1, 2, 0):
        weight_c(i, c).start()
        weight_l(i).start()

    def product(src, pair, which):
        block = full[src, rows_of(pair, DEPTH), :]
        return jnp.dot(block, wfull[which], preferred_element_type=jnp.float32).astype(jnp.bfloat16)

    def put(dest, pair, outcome):
        for h in range(heads):
            dest[h, pl.ds(pair * 2, 2)] = outcome[:, h * HD:(h + 1) * HD].reshape(2, B, HD)

    def project(src, pair):
        place = src * (blocks // 2) + pair
        put(k_s, place, product(src, pair, 1))
        put(v_s, place, product(src, pair, 2))

    def main(t, act):
        n = t // blocks + 1
        src, b = jnp.where(rising, s - n, s + n), t % blocks
        inside = (t >= 0) & (t < steps) & (src >= 0) & (src < shards)
        sent = jnp.where(rising, goes_up(s - 1, src, b), goes_down(s + 1, src, b))

        @pl.when(inside & sent)
        def _():
            act(src, b)

    def minor(t, act):
        @pl.when(inner & (t >= 0) & (t < blocks))
        def _():
            act(far, t)

    def kept(act):
        def one(src, b):
            @pl.when((src == 0) | drawable(b) | (b == 0))
            def _():
                act(src, b)

        return one

    def pass_on(src, b, act):
        @pl.when((src < s) & has_up & goes_up(s, src, b))
        def _():
            act(relay_z(src, b, 1))

        @pl.when((src > s) & has_down & goes_down(s, src, b))
        def _():
            act(relay_z(src, b, 0))

    def take_z(src, b):
        relay_z(src, b, 0).wait_recv()
        pass_on(src, b, lambda copy: copy.start())

    def take_main(src, b):
        take_z(src, b)
        relay_x(src, b, x).start()

    def take_x(src, b):
        relay_x(src, b, 1 - x).wait_recv()
        relay_c(src, b, c).start()

    def take_f(src, b):
        landed_f(b).wait_recv()
        relay_c(src, b, c).start()

    def take_c(src, b):
        relay_c(src, b, 1 - c).wait_recv()

    def global_step(src):
        def one(h, carry):
            span = pl.ds(src * blocks, blocks)
            query, keys = g_q[h].reshape(DEPTH, HD), k_s[h, span].reshape(rows, HD)
            scores = lax.dot_general(query, keys, CONTRACT, preferred_element_type=jnp.float32) * scale
            former = g_max[h]
            peak = jnp.maximum(former, jnp.max(scores, axis=-1, keepdims=True))
            expd = jnp.exp(scores - peak[:, :1])
            kept_part = jnp.exp(former - peak)
            high = expd.astype(jnp.bfloat16)
            low = (expd - high.astype(jnp.float32)).astype(jnp.bfloat16)
            values = v_s[h, span].reshape(rows, HD)
            accum = jnp.dot(high, values, preferred_element_type=jnp.float32)
            accum += jnp.dot(low, values, preferred_element_type=jnp.float32)
            g_acc[h] = g_acc[h] * kept_part + accum
            g_sum[h] = g_sum[h] * kept_part + jnp.sum(expd, axis=-1, keepdims=True)
            g_max[h] = peak
            return carry

        lax.fori_loop(0, heads, one, 0)

    @pl.when(s == OWNER)
    def _():
        g_max[...] = jnp.full_like(g_max, -jnp.inf)
        g_sum[...] = jnp.zeros_like(g_sum)
        g_acc[...] = jnp.zeros_like(g_acc)

    def pairs(t):
        b = t % blocks
        n = t // blocks + 1
        src = jnp.where(rising, s - n, s + n)
        whole = (t >= 0) & (t < steps) & (b % 2 == 1) & (src >= 0) & (src < shards)
        first = jnp.where(rising, src == 0, (src == s + 1) | (s >= OWNER))

        @pl.when(whole & ((b > 1) | first))
        def _():
            project(src, b // 2)

        @pl.when(whole & (b == blocks - 1) & (s == OWNER) & (src == shards - 1))
        def _():
            global_step(src)

    def pairs_minor(t):
        @pl.when(inner & (t >= 0) & (t < blocks) & (t % 2 == 1))
        def _():
            project(far, t // 2)

        @pl.when((s == OWNER) & (t == 1))
        def _():
            put(g_q, 0, product(0, 0, 0))

        @pl.when((s == OWNER) & (t == blocks))
        def _():
            lax.fori_loop(0, shards - 1, lambda src, carry: (global_step(src), carry)[1], 0)

    def step(t, carry):
        main(t, take_main)
        minor(t, take_z)
        main(t - X_LAG, take_x)
        minor(t - blocks, kept(take_f))

        @pl.when(t == OWN_STEP)
        def _():
            own_l.wait()
            own_c(1 - c).wait_recv()
            for i in range(3):
                weight_l(i).wait()
                weight_c(i, 1 - c).wait_recv()

        @pl.when((t >= OWN_STEP) & (t < OWN_STEP + blocks // 2))
        def _():
            project(s, t - OWN_STEP)
            put(q_s, t - OWN_STEP, product(s, t - OWN_STEP, 0))

        main(t - C_LAG, take_c)
        pairs(t - C_LAG)
        minor(t - blocks - M_LAG, kept(take_c))
        pairs_minor(t - blocks - M_LAG)
        return carry

    lax.fori_loop(0, steps + C_LAG, step, 0)

    @pl.when(s == OWNER)
    def _():
        for h in range(heads):
            g_out[:, h * HD:(h + 1) * HD] = (g_acc[h] / g_sum[h]).astype(jnp.bfloat16)
        result().start()

    col = lax.broadcasted_iota(jnp.int32, (1, (5 + R) * B), 1)

    def attend(h, carry):
        for j in range(blocks):
            g = s * blocks + j
            picks = [jnp.clip(g + d, 0, total - 1) for d in (-1, 0, 1)] + [0, 1]
            for r in range(R):
                peer = jnp.bitwise_xor(s, mask_ref[r])
                picks.append(peer * blocks + table_ref[r, h, g])
            keys = jnp.concatenate([k_s[h, p] for p in picks], axis=0)
            values = jnp.concatenate([v_s[h, p] for p in picks], axis=0)
            query = q_s[h, j]
            scores = lax.dot_general(query, keys, CONTRACT, preferred_element_type=jnp.float32) * scale
            place = g - 1 + col // B
            bias = jnp.where((col >= 3 * B) | ((place >= 2) & (place < total)), 0.0, -jnp.inf)
            scores = scores + bias
            expd = jnp.exp(scores - jnp.max(scores, axis=-1, keepdims=True))
            row_total = jnp.sum(expd, axis=-1, keepdims=True)
            out = jnp.dot(expd.astype(jnp.bfloat16), values, preferred_element_type=jnp.float32)
            o_ref[j * B:(j + 1) * B, pl.ds(pl.multiple_of(h * HD, HD), HD)] = (out / row_total).astype(jnp.bfloat16)
        return carry

    lax.fori_loop(0, heads, attend, 0)

    @pl.when(s == OWNER - 1)
    def _():
        result().wait_recv()
        o_ref[:DEPTH, :] = g_in[...]

    @pl.when(s == OWNER)
    def _():
        result().wait_send()

    own_c(c).wait_send()
    for i in range(3):
        weight_c(i, c).wait_send()
    own_sends(lambda copy: copy.wait_send())

    def sent_main(src, b):
        pass_on(src, b, lambda copy: copy.wait_send())
        relay_x(src, b, x).wait_send()
        relay_c(src, b, c).wait_send()

    def sent_z(src, b):
        pass_on(src, b, lambda copy: copy.wait_send())

    def sent_c(src, b):
        relay_c(src, b, c).wait_send()

    def drain(t, carry):
        main(t, sent_main)
        minor(t, sent_z)
        minor(t, kept(sent_c))
        return carry

    lax.fori_loop(0, steps, drain, 0)


def gathered_body(shards, tokens, projection, rand_table, round_masks):
    rows, width = tokens.shape
    mine = projection.shape[2] // 2
    heads = mine // HD
    blocks = rows // B
    dma = pltpu.SemaphoreType.DMA
    bf16, f32 = jnp.bfloat16, jnp.float32
    smem = pl.BlockSpec(memory_space=pltpu.SMEM)
    hbm = pl.BlockSpec(memory_space=pltpu.HBM)
    return pl.pallas_call(
        functools.partial(layer_kernel, shards),
        out_shape=jax.ShapeDtypeStruct((rows, mine), bf16),
        in_specs=[smem, smem, hbm, hbm],
        out_specs=pl.BlockSpec(memory_space=pltpu.VMEM),
        scratch_shapes=[
            pltpu.VMEM((shards, rows, 2 * width), bf16),
            pltpu.VMEM((3, 2 * width, mine), bf16),
            pltpu.VMEM((heads, blocks, B, HD), bf16),
            pltpu.VMEM((heads, shards * blocks, B, HD), bf16),
            pltpu.VMEM((heads, shards * blocks, B, HD), bf16),
            pltpu.VMEM((heads, 2, B, HD), bf16),
            pltpu.VMEM((heads, DEPTH, HD), f32),
            pltpu.VMEM((heads, DEPTH, HD), f32),
            pltpu.VMEM((heads, DEPTH, HD), f32),
            pltpu.VMEM((DEPTH, mine), bf16),
            pltpu.VMEM((DEPTH, mine), bf16),
            dma((2, shards, blocks)),
            dma((shards, blocks)),
            dma((blocks,)),
            dma((blocks,)),
            dma((shards, blocks)),
            dma((shards, blocks)),
            dma((shards, blocks)),
            dma((shards, blocks)),
            dma((4,)),
            dma((4,)),
            dma((4,)),
            dma((2,)),
        ],
        compiler_params=pltpu.CompilerParams(
            collective_id=0, has_side_effects=True, vmem_limit_bytes=60 * 1024 * 1024
        ),
        name="layer",
    )(jnp.transpose(rand_table, (2, 0, 1)), round_masks, tokens, jnp.transpose(projection, (1, 0, 2)))


def solution(mesh):
    shards = mesh.shape["seq"]
    few = shards == R + 1 and mesh.shape["head"] == 2
    return jax.shard_map(
        functools.partial(gathered_body, shards) if few else body,
        mesh=mesh,
        in_specs=(
            P(("grp", "seq"), "rep"),
            P("rep", None, "head"),
            P(("head", "rep"), None, None),
            P(),
        ),
        out_specs=P(("grp", "seq"), ("head", "rep")),
        check_vma=False,
    )
```

```python
import functools

import jax
import jax.numpy as jnp
from jax import lax
from jax.experimental import pallas as pl
from jax.experimental.pallas import tpu as pltpu
from jax.sharding import PartitionSpec as P

HD = 128
B = 64
R = 3


def with_halo(block, sides, width):
    for axis, dim in sides:
        count = lax.axis_size(axis)
        forward = [(i, i + 1) for i in range(count - 1)]
        backward = [(target, source) for source, target in forward]
        low = lax.ppermute(
            lax.slice_in_dim(block, block.shape[dim] - width, None, axis=dim), axis, forward
        )
        high = lax.ppermute(lax.slice_in_dim(block, 0, width, axis=dim), axis, backward)
        block = jnp.concatenate([low, block, high], axis=dim)
    return block


def spread(shard, axis, root):
    mine = lax.axis_index(axis) == root
    return lax.psum(jnp.where(mine, shard, jnp.zeros_like(shard)), axis)


def from_partner(block, axis, apart):
    count = lax.axis_size(axis)
    route = []
    for low in range(count):
        high = low | 1 << apart
        if high != low and high < count:
            route += [(low, high), (high, low)]
    return lax.ppermute(block, axis, route)


def combined_all(part, axis, combine):
    gathered = jax.tree.map(lambda a: lax.all_gather(a, axis), part)

    def take(source):
        return jax.tree.map(lambda a: lax.dynamic_index_in_dim(a, source, 0, False), gathered)

    return lax.fori_loop(
        1, lax.axis_size(axis), lambda source, state: combine(state, take(source)), take(0)
    )


def combine_parts(former, latter):
    peak = jnp.maximum(former[0], latter[0])
    former_scale = jnp.exp(former[0] - peak)
    latter_scale = jnp.exp(latter[0] - peak)
    summed = former[1] * former_scale + latter[1] * latter_scale
    accum = former[2] * former_scale[..., None] + latter[2] * latter_scale[..., None]
    return (peak, summed, accum)


def take_blocks(source, indices):
    return jnp.take(source, indices, axis=1)


def bit_set(mask_value, bit_pos):
    return jnp.bitwise_and(jnp.right_shift(mask_value, bit_pos), 1) == 1


def body(tokens, projection, rand_table, round_masks):
    scale = HD ** (-0.5)
    tok_count = tokens.shape[0]
    width_local = tokens.shape[1]
    heads_group = projection.shape[2] // HD
    heads_here = heads_group // lax.axis_size("rep")
    blocks_here = tok_count // B
    shaped = projection.reshape(width_local, 3, heads_group, HD)
    summed = lax.psum_scatter(
        jnp.einsum("td,dshe->htse", tokens, shaped, preferred_element_type=jnp.float32),
        "rep",
        scatter_dimension=0,
        tiled=True,
    )
    mixed_rows = summed.astype(jnp.bfloat16)
    queries = mixed_rows[:, :, 0]
    key_vals = jnp.moveaxis(mixed_rows[:, :, 1:], 2, 0)
    shard_id = lax.axis_index("seq")
    shards = lax.axis_size("seq")
    total_blocks = shards * blocks_here
    padded = with_halo(key_vals, (("seq", 2),), B)
    window = jnp.stack(
        [
            padded[:, :, offset * B : offset * B + tok_count].reshape(
                2, heads_here, blocks_here, B, HD
            )
            for offset in range(3)
        ],
        axis=3,
    )
    window = window.reshape(2, heads_here, blocks_here, 3 * B, HD)
    lead_queries, lead_keys = (
        spread(queries[:, : 2 * B], "seq", 0),
        spread(key_vals[:, :, : 2 * B], "seq", 0),
    )
    global_part = jnp.broadcast_to(lead_keys[:, :, None], (2, heads_here, blocks_here, 2 * B, HD))
    blocked = key_vals.reshape(2, heads_here, blocks_here, B, HD)
    bit_count = shards.bit_length() - 1
    fetched = []
    for round_id in range(R):
        peer = jnp.bitwise_xor(shard_id, round_masks[round_id])
        wanted = lax.dynamic_slice_in_dim(
            rand_table[:, :, round_id], peer * blocks_here, blocks_here, 1
        )
        payload = jax.vmap(take_blocks, in_axes=(1, 0), out_axes=1)(blocked, wanted)
        for bit_pos in range(bit_count):
            swapped = from_partner(payload, "seq", bit_pos)
            payload = jnp.where(bit_set(round_masks[round_id], bit_pos), swapped, payload)
        fetched.append(payload)
    random_part = jnp.concatenate(fetched, axis=3)
    all_keys = jnp.concatenate([window, global_part, random_part], axis=3)
    block_ids = shard_id * blocks_here + jnp.arange(blocks_here, dtype=jnp.int32)
    nearby = block_ids[:, None] - 1 + jnp.arange(3, dtype=jnp.int32)[None, :]
    allowed = (nearby >= 2) & (nearby < total_blocks)
    allowed = jnp.repeat(allowed, B, axis=1)
    allowed = jnp.concatenate([allowed, jnp.ones((blocks_here, (2 + R) * B), dtype=bool)], axis=1)
    blocked_queries = queries.reshape(heads_here, blocks_here, B, HD)
    scores = (
        jnp.einsum(
            "hjqe,hjke->hjqk", blocked_queries, all_keys[0], preferred_element_type=jnp.float32
        )
        * scale
    )
    scores = jnp.where(allowed[None, :, None, :], scores, -jnp.inf)
    peak = jnp.max(scores, axis=-1, keepdims=True)
    expd = jnp.exp(scores - peak)
    row_total = jnp.sum(expd, axis=-1, keepdims=True)
    weights = expd.astype(jnp.bfloat16)
    regular = jnp.einsum(
        "hjqk,hjke->jqhe", weights, all_keys[1], preferred_element_type=jnp.float32
    )
    regular = regular / jnp.moveaxis(row_total, 0, 2)
    regular = regular.reshape(tok_count, heads_here, HD)
    gscores = (
        jnp.einsum("hqe,hke->hqk", lead_queries, key_vals[0], preferred_element_type=jnp.float32)
        * scale
    )
    local_peak = jnp.max(gscores, axis=-1)
    local_exp = jnp.exp(gscores - local_peak[..., None])
    local_sum = jnp.sum(local_exp, axis=-1)
    local_acc = jnp.einsum(
        "hqk,hke->hqe", local_exp, key_vals[1].astype(jnp.float32), precision=lax.Precision.HIGHEST
    )
    merged = combined_all((local_peak, local_sum, local_acc), "seq", combine_parts)
    global_rows = jnp.transpose(merged[2] / merged[1][..., None], (1, 0, 2))
    global_full = jnp.pad(global_rows, ((0, tok_count - 2 * B), (0, 0), (0, 0)))
    row_ids = jnp.arange(tok_count)
    use_global = (shard_id == 0) & (row_ids < 2 * B)
    combined = jnp.where(use_global[:, None, None], global_full, regular)
    return combined.reshape(tok_count, heads_here * HD).astype(jnp.bfloat16)


MESH = pl.DeviceIdType.MESH
DEPTH = 2 * B
OWNER = 1
X_LAG = 4
C_LAG = 6
M_LAG = 2
GLOBAL_STEP = 12
OWN_STEP = 5
CONTRACT = (((1,), (1,)), ((), ()))


def layer_kernel(
    shards, table_ref, mask_ref, tok_ref, w_ref, o_ref,
    full, wfull, q_s, k_s, v_s, g_q, g_max, g_sum, g_acc, g_out, g_in,
    g_scores, g_high, g_low, scores_s, weight_s, sum_s,
    zsend, zrecv, fsend, frecv, xsend, xrecv, csend, crecv, wsend, wrecv, lsem, gsem,
):
    s, x, c = lax.axis_index("seq"), lax.axis_index("head"), lax.axis_index("rep")
    rows, width = tok_ref.shape
    cols = width // 2
    mine = w_ref.shape[2] // 2
    heads = mine // HD
    blocks = rows // B
    total = shards * blocks
    steps = (shards - 1) * blocks
    scale = HD ** (-0.5)
    has_up, has_down = s < shards - 1, s > 0
    up, down = {"seq": s + 1}, {"seq": s - 1}
    across, core = {"head": 1 - x}, {"rep": 1 - c}
    rising = s >= shards // 2
    inner = has_up & has_down
    far = jnp.where(rising, shards - 1, 0)

    barrier = pltpu.get_barrier_semaphore()

    def greet(device):
        pl.semaphore_signal(barrier, inc=1, device_id=device, device_id_type=MESH)

    greet(across)
    greet(core)

    @pl.when(has_up)
    def _():
        greet(up)

    @pl.when(has_down)
    def _():
        greet(down)

    def remote(src, dst, send, recv, device):
        return pltpu.make_async_remote_copy(
            src_ref=src, dst_ref=dst, send_sem=send, recv_sem=recv, device_id=device, device_id_type=MESH
        )

    def rows_of(i, size=B):
        return pl.ds(pl.multiple_of(i * size, size), size)

    def quarter(i):
        return pl.ds(pl.multiple_of(c * width + i * cols, cols), cols)

    def half(i):
        return pl.ds(pl.multiple_of(i * width, width), width)

    def drawable(b):
        return (b >= 2) & (b < blocks - 1)

    def goes_up(at, src, b):
        return drawable(b) | ((b < 2) & (src == 0)) | ((b == blocks - 1) & (src == at))

    def goes_down(at, src, b):
        return drawable(b) | ((b == 0) & (src == at)) | (at > OWNER)

    def own_z(i, way):
        piece = tok_ref.at[rows_of(i), pl.ds(pl.multiple_of(x * cols, cols), cols)]
        return remote(piece, full.at[s, rows_of(i), quarter(x)], zsend.at[way, s, i], zrecv.at[s, i], (down, up)[way])

    def own_f(i, way):
        piece = tok_ref.at[rows_of(i), pl.ds(pl.multiple_of((1 - x) * cols, cols), cols)]
        return remote(piece, full.at[s, rows_of(i), quarter(1 - x)], fsend.at[i], frecv.at[i], (down, up)[way])

    def relay_z(src, i, way):
        piece = full.at[src, rows_of(i), quarter(x)]
        return remote(piece, piece, zsend.at[way, src, i], zrecv.at[src, i], (down, up)[way])

    def landed_f(i):
        piece = full.at[far, rows_of(i), quarter(1 - x)]
        return remote(piece, piece, fsend.at[i], frecv.at[i], down)

    def relay_x(src, i, which):
        piece = full.at[src, rows_of(i), quarter(which)]
        return remote(piece, piece, xsend.at[src, i], xrecv.at[src, i], across)

    def relay_c(src, i, which):
        piece = full.at[src, rows_of(i), half(which)]
        return remote(piece, piece, csend.at[src, i], crecv.at[src, i], core)

    def own_c(which):
        return remote(tok_ref, full.at[s, :, half(which)], wsend.at[3], wrecv.at[3], core)

    def weight_c(i, which):
        theirs = w_ref.at[i, :, pl.ds(pl.multiple_of((1 - c) * mine, mine), mine)]
        return remote(theirs, wfull.at[i, half(which), :], wsend.at[i], wrecv.at[i], core)

    def weight_l(i):
        own = w_ref.at[i, :, pl.ds(pl.multiple_of(c * mine, mine), mine)]
        return pltpu.make_async_copy(own, wfull.at[i, half(c), :], lsem.at[i])

    own_l = pltpu.make_async_copy(tok_ref, full.at[s, :, half(c)], lsem.at[3])

    def result():
        return remote(g_out, g_in, gsem.at[0], gsem.at[1], {"seq": OWNER - 1})

    def near(b):
        return drawable(b) | (b == 0) | (s < shards - 1)

    def own_sends(act):
        def one(i, carry):
            @pl.when(has_up & goes_up(s, s, i))
            def _():
                act(own_z(i, 1))

            @pl.when(has_down & goes_down(s, s, i))
            def _():
                act(own_z(i, 0))

            return carry

        lax.fori_loop(0, blocks, one, 0)

        def other(i, carry):
            @pl.when(s == 0)
            def _():
                act(own_f(i, 1))

            @pl.when((s == shards - 1) & (drawable(i) | (i == 0)))
            def _():
                act(own_f(i, 0))

            return carry

        lax.fori_loop(0, blocks, other, 0)

    own_l.start()
    for i in (1, 2, 0):
        weight_l(i).start()
    pl.semaphore_wait(barrier, 2 + has_up.astype(jnp.int32) + has_down.astype(jnp.int32))
    own_sends(lambda copy: copy.start())
    own_c(c).start()
    for i in (1, 2, 0):
        weight_c(i, c).start()

    def product(src, pair, which):
        block = full[src, rows_of(pair, DEPTH), :]
        return jnp.dot(block, wfull[which], preferred_element_type=jnp.float32).astype(jnp.bfloat16)

    def put(dest, pair, outcome):
        for h in range(heads):
            dest[h, pl.ds(pair * 2, 2)] = outcome[:, h * HD:(h + 1) * HD].reshape(2, B, HD)

    def project(src, pair):
        place = src * (blocks // 2) + pair
        put(k_s, place, product(src, pair, 1))
        put(v_s, place, product(src, pair, 2))

    def main(t, act):
        n = t // blocks + 1
        src, b = jnp.where(rising, s - n, s + n), t % blocks
        inside = (t >= 0) & (t < steps) & (src >= 0) & (src < shards)
        sent = jnp.where(rising, goes_up(s - 1, src, b), goes_down(s + 1, src, b))

        @pl.when(inside & sent)
        def _():
            act(src, b)

    def minor(t, act):
        @pl.when(inner & (t >= 0) & (t < blocks))
        def _():
            act(far, t)

    def kept(act):
        def one(src, b):
            @pl.when((src == 0) | drawable(b) | (b == 0))
            def _():
                act(src, b)

        return one

    def pass_on(src, b, act):
        @pl.when((src < s) & has_up & goes_up(s, src, b))
        def _():
            act(relay_z(src, b, 1))

        @pl.when((src > s) & has_down & goes_down(s, src, b))
        def _():
            act(relay_z(src, b, 0))

    def take_z(src, b):
        relay_z(src, b, 0).wait_recv()
        pass_on(src, b, lambda copy: copy.start())

    def take_main(src, b):
        take_z(src, b)
        relay_x(src, b, x).start()

    def take_x(src, b):
        relay_x(src, b, 1 - x).wait_recv()
        relay_c(src, b, c).start()

    def take_f(src, b):
        landed_f(b).wait_recv()
        relay_c(src, b, c).start()

    def take_c(src, b):
        relay_c(src, b, 1 - c).wait_recv()

    def global_step(src):
        span = pl.ds(src * blocks, blocks)
        for h in range(heads):
            query, keys = g_q[h].reshape(DEPTH, HD), k_s[h, span].reshape(rows, HD)
            g_scores[h] = lax.dot_general(query, keys, CONTRACT, preferred_element_type=jnp.float32)
        for h in range(heads):
            scores = g_scores[h] * scale
            former = g_max[h]
            peak = jnp.maximum(former, jnp.max(scores, axis=-1, keepdims=True))
            expd = jnp.exp(scores - peak[:, :1])
            rest = jnp.exp(former - peak)
            high = expd.astype(jnp.bfloat16)
            g_high[h] = high
            g_low[h] = (expd - high.astype(jnp.float32)).astype(jnp.bfloat16)
            g_acc[h] = g_acc[h] * rest
            g_sum[h] = g_sum[h] * rest + jnp.sum(expd, axis=-1, keepdims=True)
            g_max[h] = peak
        for h in range(heads):
            values = v_s[h, span].reshape(rows, HD)
            accum = jnp.dot(g_high[h], values, preferred_element_type=jnp.float32)
            accum += jnp.dot(g_low[h], values, preferred_element_type=jnp.float32)
            g_acc[h] += accum

    @pl.when(s == OWNER)
    def _():
        g_max[...] = jnp.full_like(g_max, -jnp.inf)
        g_sum[...] = jnp.zeros_like(g_sum)
        g_acc[...] = jnp.zeros_like(g_acc)

    def pairs(t):
        b = t % blocks
        n = t // blocks + 1
        src = jnp.where(rising, s - n, s + n)
        whole = (t >= 0) & (t < steps) & (b % 2 == 1) & (src >= 0) & (src < shards)
        first = jnp.where(rising, src == 0, (src == s + 1) | (s >= OWNER))

        @pl.when(whole & ((b > 1) | first))
        def _():
            project(src, b // 2)

    def pairs_minor(t):
        @pl.when(inner & (t >= 0) & (t < blocks) & (t % 2 == 1))
        def _():
            project(far, t // 2)

        @pl.when((s == OWNER) & (t == 1))
        def _():
            put(g_q, 0, product(0, 0, 0))


    def step(t, carry):
        main(t, take_main)
        minor(t, take_z)
        main(t - X_LAG, take_x)
        minor(t - blocks, kept(take_f))

        @pl.when(t == OWN_STEP)
        def _():
            own_l.wait()
            own_c(1 - c).wait_recv()
            for i in range(3):
                weight_l(i).wait()
                weight_c(i, 1 - c).wait_recv()

        @pl.when((t >= OWN_STEP) & (t < OWN_STEP + blocks // 2))
        def _():
            project(s, t - OWN_STEP)
            put(q_s, t - OWN_STEP, product(s, t - OWN_STEP, 0))

        main(t - C_LAG, take_c)
        pairs(t - C_LAG)
        minor(t - blocks - M_LAG, kept(take_c))
        pairs_minor(t - blocks - M_LAG)

        n = t - GLOBAL_STEP
        @pl.when((s == OWNER) & (n >= 0) & (n % 3 == 0) & (n // 3 < shards))
        def _():
            global_step(jnp.where(n // 3 < shards - 1, (n // 3 + OWNER) % (shards - 1), shards - 1))

        return carry

    lax.fori_loop(0, steps + C_LAG, step, 0)

    @pl.when(s == OWNER)
    def _():
        for h in range(heads):
            g_out[:, h * HD:(h + 1) * HD] = (g_acc[h] / g_sum[h]).astype(jnp.bfloat16)
        result().start()

    col = lax.broadcasted_iota(jnp.int32, (1, (5 + R) * B), 1)

    def attend(h, carry):
        picks = []
        for j in range(blocks):
            g = s * blocks + j
            chosen = [jnp.clip(g + d, 0, total - 1) for d in (-1, 0, 1)] + [0, 1]
            for r in range(R):
                chosen.append(jnp.bitwise_xor(s, mask_ref[r]) * blocks + table_ref[r, h, g])
            picks.append(chosen)
        for j in range(blocks):
            keys = jnp.concatenate([k_s[h, p] for p in picks[j]], axis=0)
            scores_s[j] = lax.dot_general(q_s[h, j], keys, CONTRACT, preferred_element_type=jnp.float32)
        for j in range(blocks):
            place = s * blocks + j - 1 + col // B
            bias = jnp.where((col >= 3 * B) | ((place >= 2) & (place < total)), 0.0, -jnp.inf)
            scores = scores_s[j] * scale + bias
            expd = jnp.exp(scores - jnp.max(scores, axis=-1, keepdims=True))
            sum_s[j] = jnp.broadcast_to(jnp.sum(expd, axis=-1, keepdims=True), (B, HD))
            weight_s[j] = expd.astype(jnp.bfloat16)
        for j in range(blocks):
            values = jnp.concatenate([v_s[h, p] for p in picks[j]], axis=0)
            out = jnp.dot(weight_s[j], values, preferred_element_type=jnp.float32)
            o_ref[j * B:(j + 1) * B, pl.ds(pl.multiple_of(h * HD, HD), HD)] = (out / sum_s[j]).astype(jnp.bfloat16)
        return carry

    lax.fori_loop(0, heads, attend, 0)

    @pl.when(s == OWNER - 1)
    def _():
        result().wait_recv()
        o_ref[:DEPTH, :] = g_in[...]

    @pl.when(s == OWNER)
    def _():
        result().wait_send()

    own_c(c).wait_send()
    for i in range(3):
        weight_c(i, c).wait_send()
    own_sends(lambda copy: copy.wait_send())

    def sent_main(src, b):
        pass_on(src, b, lambda copy: copy.wait_send())
        relay_x(src, b, x).wait_send()
        relay_c(src, b, c).wait_send()

    def sent_z(src, b):
        pass_on(src, b, lambda copy: copy.wait_send())

    def sent_c(src, b):
        relay_c(src, b, c).wait_send()

    def drain(t, carry):
        main(t, sent_main)
        minor(t, sent_z)
        minor(t, kept(sent_c))
        return carry

    lax.fori_loop(0, steps, drain, 0)


def gathered_body(shards, tokens, projection, rand_table, round_masks):
    rows, width = tokens.shape
    mine = projection.shape[2] // 2
    heads = mine // HD
    blocks = rows // B
    dma = pltpu.SemaphoreType.DMA
    bf16, f32 = jnp.bfloat16, jnp.float32
    smem = pl.BlockSpec(memory_space=pltpu.SMEM)
    hbm = pl.BlockSpec(memory_space=pltpu.HBM)
    return pl.pallas_call(
        functools.partial(layer_kernel, shards),
        out_shape=jax.ShapeDtypeStruct((rows, mine), bf16),
        in_specs=[smem, smem, hbm, hbm],
        out_specs=pl.BlockSpec(memory_space=pltpu.VMEM),
        scratch_shapes=[
            pltpu.VMEM((shards, rows, 2 * width), bf16),
            pltpu.VMEM((3, 2 * width, mine), bf16),
            pltpu.VMEM((heads, blocks, B, HD), bf16),
            pltpu.VMEM((heads, shards * blocks, B, HD), bf16),
            pltpu.VMEM((heads, shards * blocks, B, HD), bf16),
            pltpu.VMEM((heads, 2, B, HD), bf16),
            pltpu.VMEM((heads, DEPTH, HD), f32),
            pltpu.VMEM((heads, DEPTH, HD), f32),
            pltpu.VMEM((heads, DEPTH, HD), f32),
            pltpu.VMEM((DEPTH, mine), bf16),
            pltpu.VMEM((DEPTH, mine), bf16),
            pltpu.VMEM((heads, DEPTH, rows), f32),
            pltpu.VMEM((heads, DEPTH, rows), bf16),
            pltpu.VMEM((heads, DEPTH, rows), bf16),
            pltpu.VMEM((blocks, B, (5 + R) * B), f32),
            pltpu.VMEM((blocks, B, (5 + R) * B), bf16),
            pltpu.VMEM((blocks, B, HD), f32),
            dma((2, shards, blocks)),
            dma((shards, blocks)),
            dma((blocks,)),
            dma((blocks,)),
            dma((shards, blocks)),
            dma((shards, blocks)),
            dma((shards, blocks)),
            dma((shards, blocks)),
            dma((4,)),
            dma((4,)),
            dma((4,)),
            dma((2,)),
        ],
        compiler_params=pltpu.CompilerParams(
            collective_id=0, has_side_effects=True, vmem_limit_bytes=60 * 1024 * 1024
        ),
        name="layer",
    )(jnp.transpose(rand_table, (2, 0, 1)), round_masks, tokens, jnp.transpose(projection, (1, 0, 2)))


def solution(mesh):
    shards = mesh.shape["seq"]
    few = shards == R + 1 and mesh.shape["head"] == 2
    return jax.shard_map(
        functools.partial(gathered_body, shards) if few else body,
        mesh=mesh,
        in_specs=(
            P(("grp", "seq"), "rep"),
            P("rep", None, "head"),
            P(("head", "rep"), None, None),
            P(),
        ),
        out_specs=P(("grp", "seq"), ("head", "rep")),
        check_vma=False,
    )
```

```python
import functools

import jax
import jax.numpy as jnp
from jax import lax
from jax.experimental import pallas as pl
from jax.experimental.pallas import tpu as pltpu
from jax.sharding import PartitionSpec as P

HD = 128
B = 64
R = 3


def with_halo(block, sides, width):
    for axis, dim in sides:
        count = lax.axis_size(axis)
        forward = [(i, i + 1) for i in range(count - 1)]
        backward = [(target, source) for source, target in forward]
        low = lax.ppermute(
            lax.slice_in_dim(block, block.shape[dim] - width, None, axis=dim), axis, forward
        )
        high = lax.ppermute(lax.slice_in_dim(block, 0, width, axis=dim), axis, backward)
        block = jnp.concatenate([low, block, high], axis=dim)
    return block


def spread(shard, axis, root):
    mine = lax.axis_index(axis) == root
    return lax.psum(jnp.where(mine, shard, jnp.zeros_like(shard)), axis)


def from_partner(block, axis, apart):
    count = lax.axis_size(axis)
    route = []
    for low in range(count):
        high = low | 1 << apart
        if high != low and high < count:
            route += [(low, high), (high, low)]
    return lax.ppermute(block, axis, route)


def combined_all(part, axis, combine):
    gathered = jax.tree.map(lambda a: lax.all_gather(a, axis), part)

    def take(source):
        return jax.tree.map(lambda a: lax.dynamic_index_in_dim(a, source, 0, False), gathered)

    return lax.fori_loop(
        1, lax.axis_size(axis), lambda source, state: combine(state, take(source)), take(0)
    )


def combine_parts(former, latter):
    peak = jnp.maximum(former[0], latter[0])
    former_scale = jnp.exp(former[0] - peak)
    latter_scale = jnp.exp(latter[0] - peak)
    summed = former[1] * former_scale + latter[1] * latter_scale
    accum = former[2] * former_scale[..., None] + latter[2] * latter_scale[..., None]
    return (peak, summed, accum)


def take_blocks(source, indices):
    return jnp.take(source, indices, axis=1)


def bit_set(mask_value, bit_pos):
    return jnp.bitwise_and(jnp.right_shift(mask_value, bit_pos), 1) == 1


def body(tokens, projection, rand_table, round_masks):
    scale = HD ** (-0.5)
    tok_count = tokens.shape[0]
    width_local = tokens.shape[1]
    heads_group = projection.shape[2] // HD
    heads_here = heads_group // lax.axis_size("rep")
    blocks_here = tok_count // B
    shaped = projection.reshape(width_local, 3, heads_group, HD)
    summed = lax.psum_scatter(
        jnp.einsum("td,dshe->htse", tokens, shaped, preferred_element_type=jnp.float32),
        "rep",
        scatter_dimension=0,
        tiled=True,
    )
    mixed_rows = summed.astype(jnp.bfloat16)
    queries = mixed_rows[:, :, 0]
    key_vals = jnp.moveaxis(mixed_rows[:, :, 1:], 2, 0)
    shard_id = lax.axis_index("seq")
    shards = lax.axis_size("seq")
    total_blocks = shards * blocks_here
    padded = with_halo(key_vals, (("seq", 2),), B)
    window = jnp.stack(
        [
            padded[:, :, offset * B : offset * B + tok_count].reshape(
                2, heads_here, blocks_here, B, HD
            )
            for offset in range(3)
        ],
        axis=3,
    )
    window = window.reshape(2, heads_here, blocks_here, 3 * B, HD)
    lead_queries, lead_keys = (
        spread(queries[:, : 2 * B], "seq", 0),
        spread(key_vals[:, :, : 2 * B], "seq", 0),
    )
    global_part = jnp.broadcast_to(lead_keys[:, :, None], (2, heads_here, blocks_here, 2 * B, HD))
    blocked = key_vals.reshape(2, heads_here, blocks_here, B, HD)
    bit_count = shards.bit_length() - 1
    fetched = []
    for round_id in range(R):
        peer = jnp.bitwise_xor(shard_id, round_masks[round_id])
        wanted = lax.dynamic_slice_in_dim(
            rand_table[:, :, round_id], peer * blocks_here, blocks_here, 1
        )
        payload = jax.vmap(take_blocks, in_axes=(1, 0), out_axes=1)(blocked, wanted)
        for bit_pos in range(bit_count):
            swapped = from_partner(payload, "seq", bit_pos)
            payload = jnp.where(bit_set(round_masks[round_id], bit_pos), swapped, payload)
        fetched.append(payload)
    random_part = jnp.concatenate(fetched, axis=3)
    all_keys = jnp.concatenate([window, global_part, random_part], axis=3)
    block_ids = shard_id * blocks_here + jnp.arange(blocks_here, dtype=jnp.int32)
    nearby = block_ids[:, None] - 1 + jnp.arange(3, dtype=jnp.int32)[None, :]
    allowed = (nearby >= 2) & (nearby < total_blocks)
    allowed = jnp.repeat(allowed, B, axis=1)
    allowed = jnp.concatenate([allowed, jnp.ones((blocks_here, (2 + R) * B), dtype=bool)], axis=1)
    blocked_queries = queries.reshape(heads_here, blocks_here, B, HD)
    scores = (
        jnp.einsum(
            "hjqe,hjke->hjqk", blocked_queries, all_keys[0], preferred_element_type=jnp.float32
        )
        * scale
    )
    scores = jnp.where(allowed[None, :, None, :], scores, -jnp.inf)
    peak = jnp.max(scores, axis=-1, keepdims=True)
    expd = jnp.exp(scores - peak)
    row_total = jnp.sum(expd, axis=-1, keepdims=True)
    weights = expd.astype(jnp.bfloat16)
    regular = jnp.einsum(
        "hjqk,hjke->jqhe", weights, all_keys[1], preferred_element_type=jnp.float32
    )
    regular = regular / jnp.moveaxis(row_total, 0, 2)
    regular = regular.reshape(tok_count, heads_here, HD)
    gscores = (
        jnp.einsum("hqe,hke->hqk", lead_queries, key_vals[0], preferred_element_type=jnp.float32)
        * scale
    )
    local_peak = jnp.max(gscores, axis=-1)
    local_exp = jnp.exp(gscores - local_peak[..., None])
    local_sum = jnp.sum(local_exp, axis=-1)
    local_acc = jnp.einsum(
        "hqk,hke->hqe", local_exp, key_vals[1].astype(jnp.float32), precision=lax.Precision.HIGHEST
    )
    merged = combined_all((local_peak, local_sum, local_acc), "seq", combine_parts)
    global_rows = jnp.transpose(merged[2] / merged[1][..., None], (1, 0, 2))
    global_full = jnp.pad(global_rows, ((0, tok_count - 2 * B), (0, 0), (0, 0)))
    row_ids = jnp.arange(tok_count)
    use_global = (shard_id == 0) & (row_ids < 2 * B)
    combined = jnp.where(use_global[:, None, None], global_full, regular)
    return combined.reshape(tok_count, heads_here * HD).astype(jnp.bfloat16)


MESH = pl.DeviceIdType.MESH
DEPTH = 2 * B
OWNER = 1
X_LAG = 4
C_LAG = 6
M_LAG = 2
GLOBAL_STEPS = (12, 18, 19, 21)
OWN_STEP = 5
LATE_STEP = 4
CONTRACT = (((1,), (1,)), ((), ()))


def layer_kernel(
    shards, table_in, mask_in, tok_ref, w_ref, o_ref,
    full, wfull, q_s, k_s, v_s, g_q, g_max, g_sum, g_acc, g_out, g_in,
    g_scores, g_high, g_low, scores_s, weight_s, sum_s,
    table_ref, mask_ref, zsend, zrecv, fsend, frecv, xsend, xrecv, csend, crecv, wsend, wrecv, lsem, gsem, tsem,
):
    s, x, c = lax.axis_index("seq"), lax.axis_index("head"), lax.axis_index("rep")
    rows, width = tok_ref.shape
    cols = width // 2
    mine = w_ref.shape[2] // 2
    heads = mine // HD
    blocks = rows // B
    total = shards * blocks
    steps = (shards - 1) * blocks
    scale = HD ** (-0.5)
    has_up, has_down = s < shards - 1, s > 0
    up, down = {"seq": s + 1}, {"seq": s - 1}
    across, core = {"head": 1 - x}, {"rep": 1 - c}
    rising = s >= shards // 2
    inner = has_up & has_down
    far = jnp.where(rising, shards - 1, 0)

    barrier = pltpu.get_barrier_semaphore()

    def greet(device):
        pl.semaphore_signal(barrier, inc=1, device_id=device, device_id_type=MESH)

    greet(across)
    greet(core)

    @pl.when(has_up)
    def _():
        greet(up)

    @pl.when(has_down)
    def _():
        greet(down)

    def remote(src, dst, send, recv, device):
        return pltpu.make_async_remote_copy(
            src_ref=src, dst_ref=dst, send_sem=send, recv_sem=recv, device_id=device, device_id_type=MESH
        )

    def rows_of(i, size=B):
        return pl.ds(pl.multiple_of(i * size, size), size)

    def quarter(i):
        return pl.ds(pl.multiple_of(c * width + i * cols, cols), cols)

    def half(i):
        return pl.ds(pl.multiple_of(i * width, width), width)

    def turn(t, upward):
        return jnp.where(upward, t % blocks, (t + 2) % blocks)

    def drawable(b):
        return (b >= 2) & (b < blocks - 1)

    def goes_up(at, src, b):
        return drawable(b) | ((b < 2) & (src == 0)) | ((b == blocks - 1) & (src == at))

    def goes_down(at, src, b):
        return drawable(b) | ((b == 0) & (src == at)) | (at > OWNER)

    def own_z(i, way):
        piece = tok_ref.at[rows_of(i), pl.ds(pl.multiple_of(x * cols, cols), cols)]
        return remote(piece, full.at[s, rows_of(i), quarter(x)], zsend.at[way, s, i], zrecv.at[s, i], (down, up)[way])

    def own_f(i, way):
        piece = tok_ref.at[rows_of(i), pl.ds(pl.multiple_of((1 - x) * cols, cols), cols)]
        return remote(piece, full.at[s, rows_of(i), quarter(1 - x)], fsend.at[i], frecv.at[i], (down, up)[way])

    def relay_z(src, i, way):
        piece = full.at[src, rows_of(i), quarter(x)]
        return remote(piece, piece, zsend.at[way, src, i], zrecv.at[src, i], (down, up)[way])

    def landed_f(i):
        piece = full.at[far, rows_of(i), quarter(1 - x)]
        return remote(piece, piece, fsend.at[i], frecv.at[i], down)

    def relay_x(src, i, which):
        piece = full.at[src, rows_of(i), quarter(which)]
        return remote(piece, piece, xsend.at[src, i], xrecv.at[src, i], across)

    def relay_c(src, i, which):
        piece = full.at[src, rows_of(i), half(which)]
        return remote(piece, piece, csend.at[src, i], crecv.at[src, i], core)

    def own_c(which):
        return remote(tok_ref, full.at[s, :, half(which)], wsend.at[3], wrecv.at[3], core)

    def weight_c(i, which):
        theirs = w_ref.at[i, :, pl.ds(pl.multiple_of((1 - c) * mine, mine), mine)]
        return remote(theirs, wfull.at[i, half(which), :], wsend.at[i], wrecv.at[i], core)

    def weight_l(i):
        own = w_ref.at[i, :, pl.ds(pl.multiple_of(c * mine, mine), mine)]
        return pltpu.make_async_copy(own, wfull.at[i, half(c), :], lsem.at[i])

    own_l = pltpu.make_async_copy(tok_ref, full.at[s, :, half(c)], lsem.at[3])

    def result():
        return remote(g_out, g_in, gsem.at[0], gsem.at[1], {"seq": OWNER - 1})

    def near(b):
        return drawable(b) | (b == 0) | (s < shards - 1)

    def urgent(b):
        return drawable(b) | (b == 0)

    def own_up(act):
        def one(i, carry):
            @pl.when(has_up & goes_up(s, s, i))
            def _():
                act(own_z(i, 1))

            return carry

        lax.fori_loop(0, blocks, one, 0)

    def own_down(act, first, last):
        def one(i, carry):
            b = (i + 2) % blocks

            @pl.when(has_down & goes_down(s, s, b) & ((first & urgent(b)) | (last & ~urgent(b))))
            def _():
                act(own_z(b, 0))

            return carry

        lax.fori_loop(0, blocks, one, 0)

    def own_full(act):
        def one(i, carry):
            b = turn(i, s == 0)

            @pl.when(s == 0)
            def _():
                act(own_f(b, 1))

            @pl.when((s == shards - 1) & urgent(b))
            def _():
                act(own_f(b, 0))

            return carry

        lax.fori_loop(0, blocks, one, 0)

    tables = [
        pltpu.make_async_copy(table_in, table_ref, tsem.at[0]),
        pltpu.make_async_copy(mask_in, mask_ref, tsem.at[1]),
    ]
    for copy in tables:
        copy.start()
    own_l.start()
    for i in (1, 2, 0):
        weight_l(i).start()
    pl.semaphore_wait(barrier, 2 + has_up.astype(jnp.int32) + has_down.astype(jnp.int32))
    own_up(lambda copy: copy.start())
    own_down(lambda copy: copy.start(), True, s == shards - 1)
    own_full(lambda copy: copy.start())
    own_c(c).start()
    for i in (1, 2, 0):
        weight_c(i, c).start()

    def product(src, pair, which):
        block = full[src, rows_of(pair, DEPTH), :]
        return jnp.dot(block, wfull[which], preferred_element_type=jnp.float32).astype(jnp.bfloat16)

    def put(dest, pair, outcome):
        for h in range(heads):
            dest[h, pl.ds(pair * 2, 2)] = outcome[:, h * HD:(h + 1) * HD].reshape(2, B, HD)

    def project(src, pair):
        place = src * (blocks // 2) + pair
        put(k_s, place, product(src, pair, 1))
        put(v_s, place, product(src, pair, 2))

    def slot(t):
        n = t // blocks + 1
        src, b = jnp.where(rising, s - n, s + n), turn(t, rising)
        edge = blocks - 2
        wide = edge + blocks - 3
        late = jnp.where(t == wide, 1, jnp.where(t == wide + 1, blocks - 1, (t - wide + edge - 1) % blocks))
        own_b = jnp.where(t < edge - 1, t + 2, jnp.where(t < edge, 0, jnp.where(t < wide, t - edge + 2, late)))
        own_src = jnp.where((t < edge) | ((t >= wide) & (t < wide + 2)), OWNER + 1, shards - 1)
        own_src = jnp.where(t < (shards - 1 - OWNER) * blocks, own_src, shards)
        return jnp.where(s == OWNER, own_src, src), jnp.where(s == OWNER, own_b, b)

    def main(t, act):
        src, b = slot(t)
        inside = (t >= 0) & (t < steps) & (src >= 0) & (src < shards)
        sent = jnp.where(rising, goes_up(s - 1, src, b), goes_down(s + 1, src, b))

        @pl.when(inside & sent)
        def _():
            act(src, b)

    def minor(t, act):
        @pl.when(inner & (t >= 0) & (t < blocks))
        def _():
            act(far, turn(t, ~rising))

    def kept(act):
        def one(src, b):
            @pl.when((src == 0) | drawable(b) | (b == 0))
            def _():
                act(src, b)

        return one

    def pass_on(src, b, act):
        @pl.when((src < s) & has_up & goes_up(s, src, b))
        def _():
            act(relay_z(src, b, 1))

        @pl.when((src > s) & has_down & goes_down(s, src, b))
        def _():
            act(relay_z(src, b, 0))

    def take_z(src, b):
        relay_z(src, b, 0).wait_recv()
        pass_on(src, b, lambda copy: copy.start())

    def take_main(src, b):
        take_z(src, b)
        relay_x(src, b, x).start()

    def take_x(src, b):
        relay_x(src, b, 1 - x).wait_recv()
        relay_c(src, b, c).start()

    def take_f(src, b):
        landed_f(b).wait_recv()
        relay_c(src, b, c).start()

    def take_c(src, b):
        relay_c(src, b, 1 - c).wait_recv()

    def global_step(src):
        span = pl.ds(src * blocks, blocks)
        for h in range(heads):
            query, keys = g_q[h].reshape(DEPTH, HD), k_s[h, span].reshape(rows, HD)
            g_scores[h] = lax.dot_general(query, keys, CONTRACT, preferred_element_type=jnp.float32)
        for h in range(heads):
            scores = g_scores[h] * scale
            former = g_max[h]
            peak = jnp.maximum(former, jnp.max(scores, axis=-1, keepdims=True))
            expd = jnp.exp(scores - peak[:, :1])
            rest = jnp.exp(former - peak)
            high = expd.astype(jnp.bfloat16)
            g_high[h] = high
            g_low[h] = (expd - high.astype(jnp.float32)).astype(jnp.bfloat16)
            g_acc[h] = g_acc[h] * rest
            g_sum[h] = g_sum[h] * rest + jnp.sum(expd, axis=-1, keepdims=True)
            g_max[h] = peak
        for h in range(heads):
            values = v_s[h, span].reshape(rows, HD)
            accum = jnp.dot(g_high[h], values, preferred_element_type=jnp.float32)
            accum += jnp.dot(g_low[h], values, preferred_element_type=jnp.float32)
            g_acc[h] += accum

    @pl.when(s == OWNER)
    def _():
        g_max[...] = jnp.full_like(g_max, -jnp.inf)
        g_sum[...] = jnp.zeros_like(g_sum)
        g_acc[...] = jnp.zeros_like(g_acc)

    def pairs(t):
        src, b = slot(t)
        whole = (t >= 0) & (t < steps) & (b % 2 == 1) & (src >= 0) & (src < shards)
        first = jnp.where(rising, src == 0, (src == s + 1) | (s >= OWNER))

        @pl.when(whole & ((b > 1) | first))
        def _():
            project(src, b // 2)

    def pairs_minor(t):
        @pl.when(inner & (t >= 0) & (t < blocks) & (t % 2 == 1))
        def _():
            project(far, turn(t, ~rising) // 2)

        @pl.when((s == OWNER) & (t == 1))
        def _():
            put(g_q, 0, product(0, 0, 0))


    def step(t, carry):
        main(t, take_main)
        minor(t, take_z)

        @pl.when((t == LATE_STEP) & (s < shards - 1))
        def _():
            own_down(lambda copy: copy.start(), False, True)

        main(t - X_LAG, take_x)
        minor(t - blocks, kept(take_f))

        @pl.when(t == OWN_STEP)
        def _():
            own_l.wait()
            own_c(1 - c).wait_recv()
            for i in range(3):
                weight_l(i).wait()
                weight_c(i, 1 - c).wait_recv()

        @pl.when((t >= OWN_STEP) & (t < OWN_STEP + blocks // 2))
        def _():
            project(s, t - OWN_STEP)
            put(q_s, t - OWN_STEP, product(s, t - OWN_STEP, 0))

        main(t - C_LAG, take_c)
        pairs(t - C_LAG)
        minor(t - blocks - M_LAG, kept(take_c))
        pairs_minor(t - blocks - M_LAG)

        due = (t == GLOBAL_STEPS[0]) | (t == GLOBAL_STEPS[1]) | (t == GLOBAL_STEPS[2]) | (t == GLOBAL_STEPS[3])

        @pl.when((s == OWNER) & due)
        def _():
            early = jnp.where(t == GLOBAL_STEPS[0], 1, 0)
            global_step(jnp.where(t < GLOBAL_STEPS[2], early, jnp.where(t == GLOBAL_STEPS[2], 2, 3)))

        return carry

    lax.fori_loop(0, steps + C_LAG, step, 0)

    @pl.when(s == OWNER)
    def _():
        for h in range(heads):
            g_out[:, h * HD:(h + 1) * HD] = (g_acc[h] / g_sum[h]).astype(jnp.bfloat16)
        result().start()

    for copy in tables:
        copy.wait()
    col = lax.broadcasted_iota(jnp.int32, (1, (5 + R) * B), 1)

    def attend(h, carry):
        picks = []
        for j in range(blocks):
            g = s * blocks + j
            chosen = [jnp.clip(g + d, 0, total - 1) for d in (-1, 0, 1)] + [0, 1]
            for r in range(R):
                chosen.append(jnp.bitwise_xor(s, mask_ref[r]) * blocks + table_ref[r, h, g])
            picks.append(chosen)
        for j in range(blocks):
            keys = jnp.concatenate([k_s[h, p] for p in picks[j]], axis=0)
            scores_s[j] = lax.dot_general(q_s[h, j], keys, CONTRACT, preferred_element_type=jnp.float32)
        for j in range(blocks):
            place = s * blocks + j - 1 + col // B
            bias = jnp.where((col >= 3 * B) | ((place >= 2) & (place < total)), 0.0, -jnp.inf)
            scores = scores_s[j] * scale + bias
            expd = jnp.exp(scores - jnp.max(scores, axis=-1, keepdims=True))
            sum_s[j] = jnp.broadcast_to(jnp.sum(expd, axis=-1, keepdims=True), (B, HD))
            weight_s[j] = expd.astype(jnp.bfloat16)
        for j in range(blocks):
            values = jnp.concatenate([v_s[h, p] for p in picks[j]], axis=0)
            out = jnp.dot(weight_s[j], values, preferred_element_type=jnp.float32)
            o_ref[j * B:(j + 1) * B, pl.ds(pl.multiple_of(h * HD, HD), HD)] = (out / sum_s[j]).astype(jnp.bfloat16)
        return carry

    lax.fori_loop(0, heads, attend, 0)

    @pl.when(s == OWNER - 1)
    def _():
        result().wait_recv()
        o_ref[:DEPTH, :] = g_in[...]

    @pl.when(s == OWNER)
    def _():
        result().wait_send()

    own_c(c).wait_send()
    for i in range(3):
        weight_c(i, c).wait_send()
    own_up(lambda copy: copy.wait_send())
    own_down(lambda copy: copy.wait_send(), True, True)
    own_full(lambda copy: copy.wait_send())

    def sent_main(src, b):
        pass_on(src, b, lambda copy: copy.wait_send())
        relay_x(src, b, x).wait_send()
        relay_c(src, b, c).wait_send()

    def sent_z(src, b):
        pass_on(src, b, lambda copy: copy.wait_send())

    def sent_c(src, b):
        relay_c(src, b, c).wait_send()

    def drain(t, carry):
        main(t, sent_main)
        minor(t, sent_z)
        minor(t, kept(sent_c))
        return carry

    lax.fori_loop(0, steps, drain, 0)


def gathered_body(shards, tokens, projection, rand_table, round_masks):
    rows, width = tokens.shape
    mine = projection.shape[2] // 2
    heads = mine // HD
    blocks = rows // B
    dma = pltpu.SemaphoreType.DMA
    bf16, f32 = jnp.bfloat16, jnp.float32
    hbm = pl.BlockSpec(memory_space=pltpu.HBM)
    return pl.pallas_call(
        functools.partial(layer_kernel, shards),
        out_shape=jax.ShapeDtypeStruct((rows, mine), bf16),
        in_specs=[hbm, hbm, hbm, hbm],
        out_specs=pl.BlockSpec(memory_space=pltpu.VMEM),
        scratch_shapes=[
            pltpu.VMEM((shards, rows, 2 * width), bf16),
            pltpu.VMEM((3, 2 * width, mine), bf16),
            pltpu.VMEM((heads, blocks, B, HD), bf16),
            pltpu.VMEM((heads, shards * blocks, B, HD), bf16),
            pltpu.VMEM((heads, shards * blocks, B, HD), bf16),
            pltpu.VMEM((heads, 2, B, HD), bf16),
            pltpu.VMEM((heads, DEPTH, HD), f32),
            pltpu.VMEM((heads, DEPTH, HD), f32),
            pltpu.VMEM((heads, DEPTH, HD), f32),
            pltpu.VMEM((DEPTH, mine), bf16),
            pltpu.VMEM((DEPTH, mine), bf16),
            pltpu.VMEM((heads, DEPTH, rows), f32),
            pltpu.VMEM((heads, DEPTH, rows), bf16),
            pltpu.VMEM((heads, DEPTH, rows), bf16),
            pltpu.VMEM((blocks, B, (5 + R) * B), f32),
            pltpu.VMEM((blocks, B, (5 + R) * B), bf16),
            pltpu.VMEM((blocks, B, HD), f32),
            pltpu.SMEM((R, heads, shards * blocks), jnp.int32),
            pltpu.SMEM((R,), jnp.int32),
            dma((2, shards, blocks)),
            dma((shards, blocks)),
            dma((blocks,)),
            dma((blocks,)),
            dma((shards, blocks)),
            dma((shards, blocks)),
            dma((shards, blocks)),
            dma((shards, blocks)),
            dma((4,)),
            dma((4,)),
            dma((4,)),
            dma((2,)),
            dma((2,)),
        ],
        compiler_params=pltpu.CompilerParams(
            collective_id=0, has_side_effects=True, vmem_limit_bytes=60 * 1024 * 1024
        ),
        name="layer",
    )(jnp.transpose(rand_table, (2, 0, 1)), round_masks, tokens, jnp.transpose(projection, (1, 0, 2)))


def solution(mesh):
    shards = mesh.shape["seq"]
    few = shards == R + 1 and mesh.shape["head"] == 2
    return jax.shard_map(
        functools.partial(gathered_body, shards) if few else body,
        mesh=mesh,
        in_specs=(
            P(("grp", "seq"), "rep"),
            P("rep", None, "head"),
            P(("head", "rep"), None, None),
            P(),
        ),
        out_specs=P(("grp", "seq"), ("head", "rep")),
        check_vma=False,
    )
```

```python
import functools

import jax
import jax.numpy as jnp
from jax import lax
from jax.experimental import pallas as pl
from jax.experimental.pallas import tpu as pltpu
from jax.sharding import PartitionSpec as P

HD = 128
B = 64
R = 3


def with_halo(block, sides, width):
    for axis, dim in sides:
        count = lax.axis_size(axis)
        forward = [(i, i + 1) for i in range(count - 1)]
        backward = [(target, source) for source, target in forward]
        low = lax.ppermute(
            lax.slice_in_dim(block, block.shape[dim] - width, None, axis=dim), axis, forward
        )
        high = lax.ppermute(lax.slice_in_dim(block, 0, width, axis=dim), axis, backward)
        block = jnp.concatenate([low, block, high], axis=dim)
    return block


def spread(shard, axis, root):
    mine = lax.axis_index(axis) == root
    return lax.psum(jnp.where(mine, shard, jnp.zeros_like(shard)), axis)


def from_partner(block, axis, apart):
    count = lax.axis_size(axis)
    route = []
    for low in range(count):
        high = low | 1 << apart
        if high != low and high < count:
            route += [(low, high), (high, low)]
    return lax.ppermute(block, axis, route)


def combined_all(part, axis, combine):
    gathered = jax.tree.map(lambda a: lax.all_gather(a, axis), part)

    def take(source):
        return jax.tree.map(lambda a: lax.dynamic_index_in_dim(a, source, 0, False), gathered)

    return lax.fori_loop(
        1, lax.axis_size(axis), lambda source, state: combine(state, take(source)), take(0)
    )


def combine_parts(former, latter):
    peak = jnp.maximum(former[0], latter[0])
    former_scale = jnp.exp(former[0] - peak)
    latter_scale = jnp.exp(latter[0] - peak)
    summed = former[1] * former_scale + latter[1] * latter_scale
    accum = former[2] * former_scale[..., None] + latter[2] * latter_scale[..., None]
    return (peak, summed, accum)


def take_blocks(source, indices):
    return jnp.take(source, indices, axis=1)


def bit_set(mask_value, bit_pos):
    return jnp.bitwise_and(jnp.right_shift(mask_value, bit_pos), 1) == 1


def body(tokens, projection, rand_table, round_masks):
    scale = HD ** (-0.5)
    tok_count = tokens.shape[0]
    width_local = tokens.shape[1]
    heads_group = projection.shape[2] // HD
    heads_here = heads_group // lax.axis_size("rep")
    blocks_here = tok_count // B
    shaped = projection.reshape(width_local, 3, heads_group, HD)
    summed = lax.psum_scatter(
        jnp.einsum("td,dshe->htse", tokens, shaped, preferred_element_type=jnp.float32),
        "rep",
        scatter_dimension=0,
        tiled=True,
    )
    mixed_rows = summed.astype(jnp.bfloat16)
    queries = mixed_rows[:, :, 0]
    key_vals = jnp.moveaxis(mixed_rows[:, :, 1:], 2, 0)
    shard_id = lax.axis_index("seq")
    shards = lax.axis_size("seq")
    total_blocks = shards * blocks_here
    padded = with_halo(key_vals, (("seq", 2),), B)
    window = jnp.stack(
        [
            padded[:, :, offset * B : offset * B + tok_count].reshape(
                2, heads_here, blocks_here, B, HD
            )
            for offset in range(3)
        ],
        axis=3,
    )
    window = window.reshape(2, heads_here, blocks_here, 3 * B, HD)
    lead_queries, lead_keys = (
        spread(queries[:, : 2 * B], "seq", 0),
        spread(key_vals[:, :, : 2 * B], "seq", 0),
    )
    global_part = jnp.broadcast_to(lead_keys[:, :, None], (2, heads_here, blocks_here, 2 * B, HD))
    blocked = key_vals.reshape(2, heads_here, blocks_here, B, HD)
    bit_count = shards.bit_length() - 1
    fetched = []
    for round_id in range(R):
        peer = jnp.bitwise_xor(shard_id, round_masks[round_id])
        wanted = lax.dynamic_slice_in_dim(
            rand_table[:, :, round_id], peer * blocks_here, blocks_here, 1
        )
        payload = jax.vmap(take_blocks, in_axes=(1, 0), out_axes=1)(blocked, wanted)
        for bit_pos in range(bit_count):
            swapped = from_partner(payload, "seq", bit_pos)
            payload = jnp.where(bit_set(round_masks[round_id], bit_pos), swapped, payload)
        fetched.append(payload)
    random_part = jnp.concatenate(fetched, axis=3)
    all_keys = jnp.concatenate([window, global_part, random_part], axis=3)
    block_ids = shard_id * blocks_here + jnp.arange(blocks_here, dtype=jnp.int32)
    nearby = block_ids[:, None] - 1 + jnp.arange(3, dtype=jnp.int32)[None, :]
    allowed = (nearby >= 2) & (nearby < total_blocks)
    allowed = jnp.repeat(allowed, B, axis=1)
    allowed = jnp.concatenate([allowed, jnp.ones((blocks_here, (2 + R) * B), dtype=bool)], axis=1)
    blocked_queries = queries.reshape(heads_here, blocks_here, B, HD)
    scores = (
        jnp.einsum(
            "hjqe,hjke->hjqk", blocked_queries, all_keys[0], preferred_element_type=jnp.float32
        )
        * scale
    )
    scores = jnp.where(allowed[None, :, None, :], scores, -jnp.inf)
    peak = jnp.max(scores, axis=-1, keepdims=True)
    expd = jnp.exp(scores - peak)
    row_total = jnp.sum(expd, axis=-1, keepdims=True)
    weights = expd.astype(jnp.bfloat16)
    regular = jnp.einsum(
        "hjqk,hjke->jqhe", weights, all_keys[1], preferred_element_type=jnp.float32
    )
    regular = regular / jnp.moveaxis(row_total, 0, 2)
    regular = regular.reshape(tok_count, heads_here, HD)
    gscores = (
        jnp.einsum("hqe,hke->hqk", lead_queries, key_vals[0], preferred_element_type=jnp.float32)
        * scale
    )
    local_peak = jnp.max(gscores, axis=-1)
    local_exp = jnp.exp(gscores - local_peak[..., None])
    local_sum = jnp.sum(local_exp, axis=-1)
    local_acc = jnp.einsum(
        "hqk,hke->hqe", local_exp, key_vals[1].astype(jnp.float32), precision=lax.Precision.HIGHEST
    )
    merged = combined_all((local_peak, local_sum, local_acc), "seq", combine_parts)
    global_rows = jnp.transpose(merged[2] / merged[1][..., None], (1, 0, 2))
    global_full = jnp.pad(global_rows, ((0, tok_count - 2 * B), (0, 0), (0, 0)))
    row_ids = jnp.arange(tok_count)
    use_global = (shard_id == 0) & (row_ids < 2 * B)
    combined = jnp.where(use_global[:, None, None], global_full, regular)
    return combined.reshape(tok_count, heads_here * HD).astype(jnp.bfloat16)


MESH = pl.DeviceIdType.MESH
DEPTH = 2 * B
OWNER = 1
X_LAG = (4, 6)
C_LAG = (6, 8)
M_LAG = 2
DRAIN_LAG = 2
SETTLE = (10, 20)
GLOBAL_STEPS = (12, 15, 18, 19)
OWN_STEP = (3, 5)
CONTRACT = (((1,), (1,)), ((), ()))


def layer_kernel(
    shards, table_in, mask_in, tok_ref, w_ref, o_ref,
    full, wfull, q_s, k_s, v_s, g_q, g_max, g_sum, g_acc, g_out, g_in,
    g_scores, g_weight, scores_s, weight_s, sum_s,
    table_ref, mask_ref, zsend, zrecv, fsend, frecv, xsend, xrecv, csend, crecv, wsend, wrecv, lsem, gsem, tsem,
):
    s, x, c = lax.axis_index("seq"), lax.axis_index("head"), lax.axis_index("rep")
    rows, width = tok_ref.shape
    cols = width // 2
    mine = w_ref.shape[2] // 2
    heads = mine // HD
    blocks = rows // B
    total = shards * blocks
    steps = (shards - 1) * blocks
    scale = HD ** (-0.5)
    has_up, has_down = s < shards - 1, s > 0
    up, down = {"seq": s + 1}, {"seq": s - 1}
    across, core = {"head": 1 - x}, {"rep": 1 - c}
    rising = s >= shards // 2
    inner = has_up & has_down
    far = jnp.where(rising, shards - 1, 0)
    x_lag, c_lag = jnp.where(inner, X_LAG[0], X_LAG[1]), jnp.where(inner, C_LAG[0], C_LAG[1])
    own_step = jnp.where(rising, OWN_STEP[1], OWN_STEP[0])

    barrier = pltpu.get_barrier_semaphore()

    def greet(device):
        pl.semaphore_signal(barrier, inc=1, device_id=device, device_id_type=MESH)

    greet(across)
    greet(core)

    @pl.when(has_up)
    def _():
        greet(up)

    @pl.when(has_down)
    def _():
        greet(down)

    def remote(src, dst, send, recv, device):
        return pltpu.make_async_remote_copy(
            src_ref=src, dst_ref=dst, send_sem=send, recv_sem=recv, device_id=device, device_id_type=MESH
        )

    def rows_of(i, size=B):
        return pl.ds(pl.multiple_of(i * size, size), size)

    def quarter(i):
        return pl.ds(pl.multiple_of(c * width + i * cols, cols), cols)

    def half(i):
        return pl.ds(pl.multiple_of(i * width, width), width)

    def turn(t, upward):
        return lax.rem(jnp.where(upward, t, t + 2), blocks)

    def drawable(b):
        return (b >= 2) & (b < blocks - 1)

    def goes_up(at, src, b):
        return drawable(b) | ((b < 2) & (src == 0)) | ((b == blocks - 1) & (src == at))

    def goes_down(at, src, b):
        return drawable(b) | ((b == 0) & (src == at)) | (at > OWNER)

    def own_z(i, way):
        piece = tok_ref.at[rows_of(i), pl.ds(pl.multiple_of(x * cols, cols), cols)]
        return remote(piece, full.at[s, rows_of(i), quarter(x)], zsend.at[way, s, i], zrecv.at[s, i], (down, up)[way])

    def own_f(i, way):
        piece = tok_ref.at[rows_of(i), pl.ds(pl.multiple_of((1 - x) * cols, cols), cols)]
        return remote(piece, full.at[s, rows_of(i), quarter(1 - x)], fsend.at[i], frecv.at[i], (down, up)[way])

    def landed_f(i):
        piece = full.at[far, rows_of(i), quarter(1 - x)]
        return remote(piece, piece, fsend.at[i], frecv.at[i], down)

    def relay_x(src, i, which):
        piece = full.at[src, rows_of(i), quarter(which)]
        return remote(piece, piece, xsend.at[src, i], xrecv.at[src, i], across)

    def relay_c(src, i, which):
        piece = full.at[src, rows_of(i), half(which)]
        return remote(piece, piece, csend.at[src, i], crecv.at[src, i], core)

    def own_c(which):
        return remote(tok_ref, full.at[s, :, half(which)], wsend.at[3], wrecv.at[3], core)

    def weight_c(i, which):
        theirs = w_ref.at[i, :, pl.ds(pl.multiple_of((1 - c) * mine, mine), mine)]
        return remote(theirs, wfull.at[i, half(which), :], wsend.at[i], wrecv.at[i], core)

    def weight_l(i):
        own = w_ref.at[i, :, pl.ds(pl.multiple_of(c * mine, mine), mine)]
        return pltpu.make_async_copy(own, wfull.at[i, half(c), :], lsem.at[i])

    own_l = pltpu.make_async_copy(tok_ref, full.at[s, :, half(c)], lsem.at[3])

    def result(part):
        some = pl.ds(part * heads // 2, heads // 2)
        return remote(g_out.at[some], g_in.at[some], gsem.at[part], gsem.at[2 + part], {"seq": OWNER - 1})

    def near(b):
        return drawable(b) | (b == 0) | (s < shards - 1)

    def urgent(b):
        return drawable(b) | (b == 0)

    def own_up(act):
        def one(i, carry):
            @pl.when(has_up & goes_up(s, s, i))
            def _():
                act(own_z(i, 1))

            return carry

        lax.fori_loop(0, blocks, one, 0)

    def own_down(act):
        def one(i, carry):
            b = (i + 2) % blocks

            @pl.when(has_down & goes_down(s, s, b))
            def _():
                act(own_z(b, 0))

            return carry

        lax.fori_loop(0, blocks, one, 0)

    def own_full(act):
        def one(i, carry):
            b = turn(i, s == 0)

            @pl.when(s == 0)
            def _():
                act(own_f(b, 1))

            @pl.when((s == shards - 1) & urgent(b))
            def _():
                act(own_f(b, 0))

            return carry

        lax.fori_loop(0, blocks, one, 0)

    tables = [
        pltpu.make_async_copy(table_in, table_ref, tsem.at[0]),
        pltpu.make_async_copy(mask_in, mask_ref, tsem.at[1]),
    ]
    for copy in tables:
        copy.start()
    own_l.start()
    for i in (1, 2, 0):
        weight_l(i).start()
    pl.semaphore_wait(barrier, 2 + has_up.astype(jnp.int32) + has_down.astype(jnp.int32))
    own_up(lambda copy: copy.start())
    own_down(lambda copy: copy.start())
    own_full(lambda copy: copy.start())
    own_c(c).start()
    for i in (1, 2, 0):
        weight_c(i, c).start()

    def product(src, pair, which):
        block = full[src, rows_of(pair, DEPTH), :]
        return jnp.dot(block, wfull[which], preferred_element_type=jnp.float32).astype(jnp.bfloat16)

    def put(dest, pair, outcome):
        for h in range(heads):
            dest[h, pl.ds(pair * 2, 2)] = outcome[:, h * HD:(h + 1) * HD].reshape(2, B, HD)

    def project(src, pair):
        place = src * (blocks // 2) + pair
        put(k_s, place, product(src, pair, 1))
        put(v_s, place, product(src, pair, 2))

    span_main = jnp.where(inner, 2 * blocks, steps)
    forth = jnp.where(rising, -1, 1)
    shift = jnp.where(rising, 0, 2)
    main_way, minor_way = jnp.where(rising, 1, 0), jnp.where(rising, 0, 1)
    main_next, minor_next = {"seq": s - forth}, {"seq": s + forth}

    def slot(t):
        n = lax.div(t, blocks)
        return s + forth * (n + 1), lax.rem(t + shift, blocks)

    def main(t, act):
        src, b = slot(t)
        upward = rising & (((b < 2) & (src == 0)) | ((b == blocks - 1) & (t < blocks)))
        downward = ~rising & ((s >= OWNER) | ((b == 0) & (t < blocks)))

        @pl.when((t >= 0) & (t < span_main) & (drawable(b) | upward | downward))
        def _():
            act(src, b)

    def minor(t, act):
        @pl.when(inner & (t >= 0) & (t < blocks))
        def _():
            act(far, turn(t, ~rising))

    def kept(act):
        def one(src, b):
            @pl.when((src == 0) | drawable(b) | (b == 0))
            def _():
                act(src, b)

        return one

    def relay_on(src, i, way, device):
        piece = full.at[src, rows_of(i), quarter(x)]
        return remote(piece, piece, zsend.at[way, src, i], zrecv.at[src, i], device)

    def pass_main(src, b, act):
        @pl.when(inner & (drawable(b) | (rising & (b < 2) & (src == 0))))
        def _():
            act(relay_on(src, b, main_way, main_next))

    def pass_minor(src, b, act):
        @pl.when(rising | (b < blocks - 1))
        def _():
            act(relay_on(src, b, minor_way, minor_next))

    def take_minor(src, b):
        relay_on(src, b, 0, up).wait_recv()
        pass_minor(src, b, lambda copy: copy.start())

    def take_main(src, b):
        relay_on(src, b, 0, up).wait_recv()
        relay_x(src, b, x).start()
        pass_main(src, b, lambda copy: copy.start())

    def take_x(src, b):
        relay_x(src, b, 1 - x).wait_recv()
        relay_c(src, b, c).start()

    def take_f(src, b):
        landed_f(b).wait_recv()
        relay_c(src, b, c).start()

    def take_c(src, b):
        relay_c(src, b, 1 - c).wait_recv()

    def global_step(src, start, count, some):
        span = pl.ds(src * blocks + start, count)
        keys_here = count * B
        for h in some:
            query, keys = g_q[h].reshape(DEPTH, HD), k_s[h, span].reshape(keys_here, HD)
            g_scores[h, :, :keys_here] = lax.dot_general(query, keys, CONTRACT, preferred_element_type=jnp.float32)
        for h in some:
            scores = g_scores[h, :, :keys_here] * scale
            former = g_max[h]
            peak = jnp.maximum(former, jnp.max(scores, axis=-1, keepdims=True))
            expd = jnp.exp(scores - jnp.concatenate([peak] * (keys_here // HD), axis=1))
            rest = jnp.exp(former - peak)
            high = expd.astype(jnp.bfloat16)
            g_weight[h, :DEPTH, :keys_here] = high
            g_weight[h, DEPTH:, :keys_here] = (expd - high.astype(jnp.float32)).astype(jnp.bfloat16)
            g_acc[h] = g_acc[h] * rest
            g_sum[h] = g_sum[h] * rest + jnp.sum(expd, axis=-1, keepdims=True)
            g_max[h] = peak
        for h in some:
            values = v_s[h, span].reshape(keys_here, HD)
            accum = jnp.dot(g_weight[h, :, :keys_here], values, preferred_element_type=jnp.float32)
            g_acc[h] += accum[:DEPTH] + accum[DEPTH:]

    @pl.when(s == OWNER)
    def _():
        g_max[...] = jnp.full_like(g_max, -jnp.inf)
        g_sum[...] = jnp.zeros_like(g_sum)
        g_acc[...] = jnp.zeros_like(g_acc)

    def pairs(t):
        src, b = slot(t)
        first = jnp.where(rising, src == 0, (t < blocks) | (s >= OWNER))

        @pl.when((t >= 0) & (t < span_main) & (lax.rem(b, 2) == 1) & ((b > 1) | first))
        def _():
            project(src, lax.div(b, 2))

    def pairs_minor(t):
        @pl.when(inner & (t >= 0) & (t < blocks) & (lax.rem(t, 2) == 1))
        def _():
            project(far, lax.div(turn(t, ~rising), 2))

        @pl.when((s == OWNER) & (t == 1))
        def _():
            put(g_q, 0, product(0, 0, 0))


    def sent_main(src, b):
        pass_main(src, b, lambda copy: copy.wait_send())
        relay_x(src, b, x).wait_send()
        relay_c(src, b, c).wait_send()

    def sent_minor(src, b):
        pass_minor(src, b, lambda copy: copy.wait_send())

    def sent_c(src, b):
        relay_c(src, b, c).wait_send()

    settle = jnp.where(inner, SETTLE[0], SETTLE[1])

    def step(t, carry):
        main(t, take_main)
        minor(t, take_minor)

        main(t - x_lag, take_x)
        minor(t - blocks, kept(take_f))

        @pl.when(t == own_step)
        def _():
            own_l.wait()
            own_c(1 - c).wait_recv()
            for i in range(3):
                weight_l(i).wait()
                weight_c(i, 1 - c).wait_recv()

        @pl.when((t >= own_step) & (t < own_step + blocks // 2))
        def _():
            project(s, t - own_step)
            put(q_s, t - own_step, product(s, t - own_step, 0))

        main(t - c_lag, take_c)
        pairs(t - c_lag)
        minor(t - blocks - M_LAG, kept(take_c))
        pairs_minor(t - blocks - M_LAG)
        main(t - c_lag - DRAIN_LAG, sent_main)
        minor(t - blocks, sent_minor)
        minor(t - blocks - C_LAG[0] + 1, kept(sent_c))

        @pl.when(t == settle)
        def _():
            own_c(c).wait_send()
            for i in range(3):
                weight_c(i, c).wait_send()
            own_up(lambda copy: copy.wait_send())
            own_down(lambda copy: copy.wait_send())
            own_full(lambda copy: copy.wait_send())


        whole_due = (t == GLOBAL_STEPS[0]) | (t == GLOBAL_STEPS[1]) | (t == GLOBAL_STEPS[2])

        @pl.when((s == OWNER) & whole_due)
        def _():
            src = jnp.where(t == GLOBAL_STEPS[0], OWNER, jnp.where(t == GLOBAL_STEPS[1], OWNER + 1, 0))
            global_step(src, 0, blocks, range(heads))

        @pl.when((s == OWNER) & (t == GLOBAL_STEPS[3]))
        def _():
            global_step(shards - 1, 2, blocks // 2, range(heads))

        return carry

    lax.fori_loop(0, span_main + c_lag, step, 0)

    @pl.when(s == OWNER)
    def _():
        for part in range(2):
            some = range(part * heads // 2, (part + 1) * heads // 2)
            global_step(shards - 1, 0, 2, some)
            global_step(shards - 1, blocks - 2, 2, some)
            for h in some:
                g_out[h] = (g_acc[h] / g_sum[h]).astype(jnp.bfloat16)
            result(part).start()

    for copy in tables:
        copy.wait()
    col = lax.broadcasted_iota(jnp.int32, (1, (5 + R) * B), 1)

    def attend(h, carry):
        picks = []
        for j in range(blocks):
            g = s * blocks + j
            chosen = [jnp.clip(g + d, 0, total - 1) for d in (-1, 0, 1)] + [0, 1]
            for r in range(R):
                chosen.append(jnp.bitwise_xor(s, mask_ref[r]) * blocks + table_ref[r, h, g])
            picks.append(chosen)
        for j in range(blocks):
            keys = jnp.concatenate([k_s[h, p] for p in picks[j]], axis=0)
            scores_s[j] = lax.dot_general(q_s[h, j], keys, CONTRACT, preferred_element_type=jnp.float32)
        for j in range(blocks):
            place = s * blocks + j - 1 + col // B
            bias = jnp.where((col >= 3 * B) | ((place >= 2) & (place < total)), 0.0, -jnp.inf)
            scores = scores_s[j] * scale + bias
            expd = jnp.exp(scores - jnp.max(scores, axis=-1, keepdims=True))
            sum_s[j] = jnp.broadcast_to(jnp.sum(expd, axis=-1, keepdims=True), (B, HD))
            weight_s[j] = expd.astype(jnp.bfloat16)
        for j in range(blocks):
            values = jnp.concatenate([v_s[h, p] for p in picks[j]], axis=0)
            out = jnp.dot(weight_s[j], values, preferred_element_type=jnp.float32)
            o_ref[j * B:(j + 1) * B, pl.ds(pl.multiple_of(h * HD, HD), HD)] = (out / sum_s[j]).astype(jnp.bfloat16)
        return carry

    lax.fori_loop(0, heads, attend, 0)

    @pl.when(s == OWNER - 1)
    def _():
        for part in range(2):
            result(part).wait_recv()
        for h in range(heads):
            o_ref[:DEPTH, h * HD:(h + 1) * HD] = g_in[h]

    @pl.when(s == OWNER)
    def _():
        for part in range(2):
            result(part).wait_send()

    lax.fori_loop(span_main - DRAIN_LAG, span_main, lambda t, carry: (main(t, sent_main), carry)[1], 0)


def gathered_body(shards, tokens, projection, rand_table, round_masks):
    rows, width = tokens.shape
    mine = projection.shape[2] // 2
    heads = mine // HD
    blocks = rows // B
    dma = pltpu.SemaphoreType.DMA
    bf16, f32 = jnp.bfloat16, jnp.float32
    hbm = pl.BlockSpec(memory_space=pltpu.HBM)
    return pl.pallas_call(
        functools.partial(layer_kernel, shards),
        out_shape=jax.ShapeDtypeStruct((rows, mine), bf16),
        in_specs=[hbm, hbm, hbm, hbm],
        out_specs=pl.BlockSpec(memory_space=pltpu.VMEM),
        scratch_shapes=[
            pltpu.VMEM((shards, rows, 2 * width), bf16),
            pltpu.VMEM((3, 2 * width, mine), bf16),
            pltpu.VMEM((heads, blocks, B, HD), bf16),
            pltpu.VMEM((heads, shards * blocks, B, HD), bf16),
            pltpu.VMEM((heads, shards * blocks, B, HD), bf16),
            pltpu.VMEM((heads, 2, B, HD), bf16),
            pltpu.VMEM((heads, DEPTH, HD), f32),
            pltpu.VMEM((heads, DEPTH, HD), f32),
            pltpu.VMEM((heads, DEPTH, HD), f32),
            pltpu.VMEM((heads, DEPTH, HD), bf16),
            pltpu.VMEM((heads, DEPTH, HD), bf16),
            pltpu.VMEM((heads, DEPTH, rows), f32),
            pltpu.VMEM((heads, 2 * DEPTH, rows), bf16),
            pltpu.VMEM((blocks, B, (5 + R) * B), f32),
            pltpu.VMEM((blocks, B, (5 + R) * B), bf16),
            pltpu.VMEM((blocks, B, HD), f32),
            pltpu.SMEM((R, heads, shards * blocks), jnp.int32),
            pltpu.SMEM((R,), jnp.int32),
            dma((2, shards, blocks)),
            dma((shards, blocks)),
            dma((blocks,)),
            dma((blocks,)),
            dma((shards, blocks)),
            dma((shards, blocks)),
            dma((shards, blocks)),
            dma((shards, blocks)),
            dma((4,)),
            dma((4,)),
            dma((4,)),
            dma((4,)),
            dma((2,)),
        ],
        compiler_params=pltpu.CompilerParams(
            collective_id=0, has_side_effects=True, vmem_limit_bytes=60 * 1024 * 1024
        ),
        name="layer",
    )(jnp.transpose(rand_table, (2, 0, 1)), round_masks, tokens, jnp.transpose(projection, (1, 0, 2)))


def solution(mesh):
    shards = mesh.shape["seq"]
    few = shards == R + 1 and mesh.shape["head"] == 2
    return jax.shard_map(
        functools.partial(gathered_body, shards) if few else body,
        mesh=mesh,
        in_specs=(
            P(("grp", "seq"), "rep"),
            P("rep", None, "head"),
            P(("head", "rep"), None, None),
            P(),
        ),
        out_specs=P(("grp", "seq"), ("head", "rep")),
        check_vma=False,
    )
```

```python
import functools

import jax
import jax.numpy as jnp
from jax import lax
from jax.experimental import pallas as pl
from jax.experimental.pallas import tpu as pltpu
from jax.sharding import PartitionSpec as P

HD = 128
B = 64
R = 3


def with_halo(block, sides, width):
    for axis, dim in sides:
        count = lax.axis_size(axis)
        forward = [(i, i + 1) for i in range(count - 1)]
        backward = [(target, source) for source, target in forward]
        low = lax.ppermute(
            lax.slice_in_dim(block, block.shape[dim] - width, None, axis=dim), axis, forward
        )
        high = lax.ppermute(lax.slice_in_dim(block, 0, width, axis=dim), axis, backward)
        block = jnp.concatenate([low, block, high], axis=dim)
    return block


def spread(shard, axis, root):
    mine = lax.axis_index(axis) == root
    return lax.psum(jnp.where(mine, shard, jnp.zeros_like(shard)), axis)


def from_partner(block, axis, apart):
    count = lax.axis_size(axis)
    route = []
    for low in range(count):
        high = low | 1 << apart
        if high != low and high < count:
            route += [(low, high), (high, low)]
    return lax.ppermute(block, axis, route)


def combined_all(part, axis, combine):
    gathered = jax.tree.map(lambda a: lax.all_gather(a, axis), part)

    def take(source):
        return jax.tree.map(lambda a: lax.dynamic_index_in_dim(a, source, 0, False), gathered)

    return lax.fori_loop(
        1, lax.axis_size(axis), lambda source, state: combine(state, take(source)), take(0)
    )


def combine_parts(former, latter):
    peak = jnp.maximum(former[0], latter[0])
    former_scale = jnp.exp(former[0] - peak)
    latter_scale = jnp.exp(latter[0] - peak)
    summed = former[1] * former_scale + latter[1] * latter_scale
    accum = former[2] * former_scale[..., None] + latter[2] * latter_scale[..., None]
    return (peak, summed, accum)


def take_blocks(source, indices):
    return jnp.take(source, indices, axis=1)


def bit_set(mask_value, bit_pos):
    return jnp.bitwise_and(jnp.right_shift(mask_value, bit_pos), 1) == 1


def body(tokens, projection, rand_table, round_masks):
    scale = HD ** (-0.5)
    tok_count = tokens.shape[0]
    width_local = tokens.shape[1]
    heads_group = projection.shape[2] // HD
    heads_here = heads_group // lax.axis_size("rep")
    blocks_here = tok_count // B
    shaped = projection.reshape(width_local, 3, heads_group, HD)
    summed = lax.psum_scatter(
        jnp.einsum("td,dshe->htse", tokens, shaped, preferred_element_type=jnp.float32),
        "rep",
        scatter_dimension=0,
        tiled=True,
    )
    mixed_rows = summed.astype(jnp.bfloat16)
    queries = mixed_rows[:, :, 0]
    key_vals = jnp.moveaxis(mixed_rows[:, :, 1:], 2, 0)
    shard_id = lax.axis_index("seq")
    shards = lax.axis_size("seq")
    total_blocks = shards * blocks_here
    padded = with_halo(key_vals, (("seq", 2),), B)
    window = jnp.stack(
        [
            padded[:, :, offset * B : offset * B + tok_count].reshape(
                2, heads_here, blocks_here, B, HD
            )
            for offset in range(3)
        ],
        axis=3,
    )
    window = window.reshape(2, heads_here, blocks_here, 3 * B, HD)
    lead_queries, lead_keys = (
        spread(queries[:, : 2 * B], "seq", 0),
        spread(key_vals[:, :, : 2 * B], "seq", 0),
    )
    global_part = jnp.broadcast_to(lead_keys[:, :, None], (2, heads_here, blocks_here, 2 * B, HD))
    blocked = key_vals.reshape(2, heads_here, blocks_here, B, HD)
    bit_count = shards.bit_length() - 1
    fetched = []
    for round_id in range(R):
        peer = jnp.bitwise_xor(shard_id, round_masks[round_id])
        wanted = lax.dynamic_slice_in_dim(
            rand_table[:, :, round_id], peer * blocks_here, blocks_here, 1
        )
        payload = jax.vmap(take_blocks, in_axes=(1, 0), out_axes=1)(blocked, wanted)
        for bit_pos in range(bit_count):
            swapped = from_partner(payload, "seq", bit_pos)
            payload = jnp.where(bit_set(round_masks[round_id], bit_pos), swapped, payload)
        fetched.append(payload)
    random_part = jnp.concatenate(fetched, axis=3)
    all_keys = jnp.concatenate([window, global_part, random_part], axis=3)
    block_ids = shard_id * blocks_here + jnp.arange(blocks_here, dtype=jnp.int32)
    nearby = block_ids[:, None] - 1 + jnp.arange(3, dtype=jnp.int32)[None, :]
    allowed = (nearby >= 2) & (nearby < total_blocks)
    allowed = jnp.repeat(allowed, B, axis=1)
    allowed = jnp.concatenate([allowed, jnp.ones((blocks_here, (2 + R) * B), dtype=bool)], axis=1)
    blocked_queries = queries.reshape(heads_here, blocks_here, B, HD)
    scores = (
        jnp.einsum(
            "hjqe,hjke->hjqk", blocked_queries, all_keys[0], preferred_element_type=jnp.float32
        )
        * scale
    )
    scores = jnp.where(allowed[None, :, None, :], scores, -jnp.inf)
    peak = jnp.max(scores, axis=-1, keepdims=True)
    expd = jnp.exp(scores - peak)
    row_total = jnp.sum(expd, axis=-1, keepdims=True)
    weights = expd.astype(jnp.bfloat16)
    regular = jnp.einsum(
        "hjqk,hjke->jqhe", weights, all_keys[1], preferred_element_type=jnp.float32
    )
    regular = regular / jnp.moveaxis(row_total, 0, 2)
    regular = regular.reshape(tok_count, heads_here, HD)
    gscores = (
        jnp.einsum("hqe,hke->hqk", lead_queries, key_vals[0], preferred_element_type=jnp.float32)
        * scale
    )
    local_peak = jnp.max(gscores, axis=-1)
    local_exp = jnp.exp(gscores - local_peak[..., None])
    local_sum = jnp.sum(local_exp, axis=-1)
    local_acc = jnp.einsum(
        "hqk,hke->hqe", local_exp, key_vals[1].astype(jnp.float32), precision=lax.Precision.HIGHEST
    )
    merged = combined_all((local_peak, local_sum, local_acc), "seq", combine_parts)
    global_rows = jnp.transpose(merged[2] / merged[1][..., None], (1, 0, 2))
    global_full = jnp.pad(global_rows, ((0, tok_count - 2 * B), (0, 0), (0, 0)))
    row_ids = jnp.arange(tok_count)
    use_global = (shard_id == 0) & (row_ids < 2 * B)
    combined = jnp.where(use_global[:, None, None], global_full, regular)
    return combined.reshape(tok_count, heads_here * HD).astype(jnp.bfloat16)


MESH = pl.DeviceIdType.MESH
DEPTH = 2 * B
OWNER = 1
X_LAG = (3, 6)
C_LAG = (5, 8)
M_LAG = 2
DRAIN_LAG = 2
SETTLE = (10, 20)
GLOBAL_STEPS = (12, 14, 18, 17)
OWN_STEP = (3, 5)
CONTRACT = (((1,), (1,)), ((), ()))


def layer_kernel(
    shards, table_in, mask_in, tok_ref, w_ref, out_ref,
    o_ref, full, wfull, q_s, k_s, v_s, g_q, g_max, g_sum, g_acc, g_out, g_in,
    g_scores, g_weight, scores_s, weight_s, sum_s,
    table_ref, mask_ref, zsend, zrecv, fsend, frecv, xsend, xrecv, csend, crecv, wsend, wrecv, lsem, gsem, tsem, osem,
):
    s, x, c = lax.axis_index("seq"), lax.axis_index("head"), lax.axis_index("rep")
    rows, width = tok_ref.shape
    cols = width // 2
    mine = w_ref.shape[2] // 2
    heads = mine // HD
    blocks = rows // B
    total = shards * blocks
    steps = (shards - 1) * blocks
    scale = HD ** (-0.5)
    has_up, has_down = s < shards - 1, s > 0
    up, down = {"seq": s + 1}, {"seq": s - 1}
    across, core = {"head": 1 - x}, {"rep": 1 - c}
    rising = s >= shards // 2
    inner = has_up & has_down
    far = jnp.where(rising, shards - 1, 0)
    x_lag, c_lag = jnp.where(inner, X_LAG[0], X_LAG[1]), jnp.where(inner, C_LAG[0], C_LAG[1])
    own_step = jnp.where(rising, OWN_STEP[1], OWN_STEP[0])

    barrier = pltpu.get_barrier_semaphore()

    def greet(device):
        pl.semaphore_signal(barrier, inc=1, device_id=device, device_id_type=MESH)

    greet(across)
    greet(core)

    @pl.when(has_up)
    def _():
        greet(up)

    @pl.when(has_down)
    def _():
        greet(down)

    def remote(src, dst, send, recv, device):
        return pltpu.make_async_remote_copy(
            src_ref=src, dst_ref=dst, send_sem=send, recv_sem=recv, device_id=device, device_id_type=MESH
        )

    def rows_of(i, size=B):
        return pl.ds(pl.multiple_of(i * size, size), size)

    def quarter(i):
        return pl.ds(pl.multiple_of(c * width + i * cols, cols), cols)

    def half(i):
        return pl.ds(pl.multiple_of(i * width, width), width)

    def turn(t, upward):
        return lax.rem(jnp.where(upward, t, t + 2), blocks)

    def drawable(b):
        return (b >= 2) & (b < blocks - 1)

    def goes_up(at, src, b):
        return drawable(b) | ((b < 2) & (src == 0)) | ((b == blocks - 1) & (src == at))

    def goes_down(at, src, b):
        return drawable(b) | ((b == 0) & (src == at)) | (at > OWNER)

    def own_z(i, way):
        piece = tok_ref.at[rows_of(i), pl.ds(pl.multiple_of(x * cols, cols), cols)]
        return remote(piece, full.at[s, rows_of(i), quarter(x)], zsend.at[way, s, i], zrecv.at[s, i], (down, up)[way])

    def own_f(i, way):
        piece = tok_ref.at[rows_of(i), pl.ds(pl.multiple_of((1 - x) * cols, cols), cols)]
        return remote(piece, full.at[s, rows_of(i), quarter(1 - x)], fsend.at[i], frecv.at[i], (down, up)[way])

    def landed_f(i):
        piece = full.at[far, rows_of(i), quarter(1 - x)]
        return remote(piece, piece, fsend.at[i], frecv.at[i], down)

    def relay_x(src, i, which):
        piece = full.at[src, rows_of(i), quarter(which)]
        return remote(piece, piece, xsend.at[src, i], xrecv.at[src, i], across)

    def relay_c(src, i, which):
        piece = full.at[src, rows_of(i), half(which)]
        return remote(piece, piece, csend.at[src, i], crecv.at[src, i], core)

    def own_c(which):
        return remote(tok_ref, full.at[s, :, half(which)], wsend.at[3], wrecv.at[3], core)

    def weight_c(i, which):
        theirs = w_ref.at[i, :, pl.ds(pl.multiple_of((1 - c) * mine, mine), mine)]
        return remote(theirs, wfull.at[i, half(which), :], wsend.at[i], wrecv.at[i], core)

    def weight_l(i):
        own = w_ref.at[i, :, pl.ds(pl.multiple_of(c * mine, mine), mine)]
        return pltpu.make_async_copy(own, wfull.at[i, half(c), :], lsem.at[i])

    own_l = pltpu.make_async_copy(tok_ref, full.at[s, :, half(c)], lsem.at[3])

    def result(part):
        return remote(g_out.at[part], g_in.at[part], gsem.at[0, part], gsem.at[1, part], {"seq": OWNER - 1})

    def near(b):
        return drawable(b) | (b == 0) | (s < shards - 1)

    def urgent(b):
        return drawable(b) | (b == 0)

    def own_up(act):
        def one(i, carry):
            @pl.when(has_up & goes_up(s, s, i))
            def _():
                act(own_z(i, 1))

            return carry

        lax.fori_loop(0, blocks, one, 0)

    def own_down(act):
        def one(i, carry):
            b = (i + 2) % blocks

            @pl.when(has_down & goes_down(s, s, b))
            def _():
                act(own_z(b, 0))

            return carry

        lax.fori_loop(0, blocks, one, 0)

    def own_full(act):
        def one(i, carry):
            b = turn(i, s == 0)

            @pl.when(s == 0)
            def _():
                act(own_f(b, 1))

            @pl.when((s == shards - 1) & urgent(b))
            def _():
                act(own_f(b, 0))

            return carry

        lax.fori_loop(0, blocks, one, 0)

    tables = [
        pltpu.make_async_copy(table_in, table_ref, tsem.at[0]),
        pltpu.make_async_copy(mask_in, mask_ref, tsem.at[1]),
    ]
    for copy in tables:
        copy.start()
    own_l.start()
    for i in (1, 2, 0):
        weight_l(i).start()
    pl.semaphore_wait(barrier, 2 + has_up.astype(jnp.int32) + has_down.astype(jnp.int32))
    own_up(lambda copy: copy.start())
    own_down(lambda copy: copy.start())
    own_full(lambda copy: copy.start())
    own_c(c).start()
    for i in (1, 2, 0):
        weight_c(i, c).start()

    def product(src, pair, which):
        block = full[src, rows_of(pair, DEPTH), :]
        return jnp.dot(block, wfull[which], preferred_element_type=jnp.float32).astype(jnp.bfloat16)

    def put(dest, pair, outcome):
        for h in range(heads):
            dest[h, pl.ds(pair * 2, 2)] = outcome[:, h * HD:(h + 1) * HD].reshape(2, B, HD)

    def project(src, pair):
        place = src * (blocks // 2) + pair
        put(k_s, place, product(src, pair, 1))
        put(v_s, place, product(src, pair, 2))

    span_main = jnp.where(inner, 2 * blocks, steps)
    forth = jnp.where(rising, -1, 1)
    shift = jnp.where(rising, 0, 2)
    main_way, minor_way = jnp.where(rising, 1, 0), jnp.where(rising, 0, 1)
    main_next, minor_next = {"seq": s - forth}, {"seq": s + forth}

    def slot(t):
        n = lax.div(t, blocks)
        return s + forth * (n + 1), lax.rem(t + shift, blocks)

    def main(t, act):
        src, b = slot(t)
        upward = rising & (((b < 2) & (src == 0)) | ((b == blocks - 1) & (t < blocks)))
        downward = ~rising & ((s >= OWNER) | ((b == 0) & (t < blocks)))

        @pl.when((t >= 0) & (t < span_main) & (drawable(b) | upward | downward))
        def _():
            act(src, b)

    def minor(t, act):
        @pl.when(inner & (t >= 0) & (t < blocks))
        def _():
            act(far, turn(t, ~rising))

    def kept(act):
        def one(src, b):
            @pl.when((src == 0) | drawable(b) | (b == 0))
            def _():
                act(src, b)

        return one

    def relay_on(src, i, way, device):
        piece = full.at[src, rows_of(i), quarter(x)]
        return remote(piece, piece, zsend.at[way, src, i], zrecv.at[src, i], device)

    def pass_main(src, b, act):
        @pl.when(inner & (drawable(b) | (rising & (b < 2) & (src == 0))))
        def _():
            act(relay_on(src, b, main_way, main_next))

    def pass_minor(src, b, act):
        @pl.when(rising | (b < blocks - 1))
        def _():
            act(relay_on(src, b, minor_way, minor_next))

    def take_minor(src, b):
        relay_on(src, b, 0, up).wait_recv()
        pass_minor(src, b, lambda copy: copy.start())

    def take_main(src, b):
        relay_on(src, b, 0, up).wait_recv()
        relay_x(src, b, x).start()
        pass_main(src, b, lambda copy: copy.start())

    def take_x(src, b):
        relay_x(src, b, 1 - x).wait_recv()
        relay_c(src, b, c).start()

    def take_f(src, b):
        landed_f(b).wait_recv()
        relay_c(src, b, c).start()

    def take_c(src, b):
        relay_c(src, b, 1 - c).wait_recv()

    def global_step(src, start, count, some):
        span = pl.ds(src * blocks + start, count)
        keys_here = count * B
        for h in some:
            query, keys = g_q[h].reshape(DEPTH, HD), k_s[h, span].reshape(keys_here, HD)
            g_scores[h, :, :keys_here] = lax.dot_general(query, keys, CONTRACT, preferred_element_type=jnp.float32)
        for h in some:
            scores = g_scores[h, :, :keys_here] * scale
            former = g_max[h]
            peak = jnp.maximum(former, jnp.max(scores, axis=-1, keepdims=True))
            expd = jnp.exp(scores - jnp.concatenate([peak] * (keys_here // HD), axis=1))
            rest = jnp.exp(former - peak)
            high = expd.astype(jnp.bfloat16)
            g_weight[h, :DEPTH, :keys_here] = high
            g_weight[h, DEPTH:, :keys_here] = (expd - high.astype(jnp.float32)).astype(jnp.bfloat16)
            g_acc[h] = g_acc[h] * rest
            g_sum[h] = g_sum[h] * rest + jnp.sum(expd, axis=-1, keepdims=True)
            g_max[h] = peak
        for h in some:
            values = v_s[h, span].reshape(keys_here, HD)
            accum = jnp.dot(g_weight[h, :, :keys_here], values, preferred_element_type=jnp.float32)
            g_acc[h] += accum[:DEPTH] + accum[DEPTH:]

    @pl.when(s == OWNER)
    def _():
        g_max[...] = jnp.full_like(g_max, -jnp.inf)
        g_sum[...] = jnp.zeros_like(g_sum)
        g_acc[...] = jnp.zeros_like(g_acc)

    def pairs(t):
        src, b = slot(t)
        first = jnp.where(rising, src == 0, (t < blocks) | (s >= OWNER))

        @pl.when((t >= 0) & (t < span_main) & (lax.rem(b, 2) == 1) & ((b > 1) | first))
        def _():
            project(src, lax.div(b, 2))

    def pairs_minor(t):
        @pl.when(inner & (t >= 0) & (t < blocks) & (lax.rem(t, 2) == 1))
        def _():
            project(far, lax.div(turn(t, ~rising), 2))

        @pl.when((s == OWNER) & (t == 1))
        def _():
            put(g_q, 0, product(0, 0, 0))


    def sent_main(src, b):
        pass_main(src, b, lambda copy: copy.wait_send())
        relay_x(src, b, x).wait_send()
        relay_c(src, b, c).wait_send()

    def sent_minor(src, b):
        pass_minor(src, b, lambda copy: copy.wait_send())

    def sent_c(src, b):
        relay_c(src, b, c).wait_send()

    settle = jnp.where(inner, SETTLE[0], SETTLE[1])

    def step(t, carry):
        main(t, take_main)
        minor(t, take_minor)

        main(t - x_lag, take_x)
        minor(t - blocks, kept(take_f))

        @pl.when(t == own_step)
        def _():
            own_l.wait()
            own_c(1 - c).wait_recv()
            for i in range(3):
                weight_l(i).wait()
                weight_c(i, 1 - c).wait_recv()

        @pl.when((t >= own_step) & (t < own_step + blocks // 2))
        def _():
            project(s, t - own_step)
            put(q_s, t - own_step, product(s, t - own_step, 0))

        main(t - c_lag, take_c)
        pairs(t - c_lag)
        minor(t - blocks - M_LAG, kept(take_c))
        pairs_minor(t - blocks - M_LAG)
        main(t - c_lag - DRAIN_LAG, sent_main)
        minor(t - blocks, sent_minor)
        minor(t - blocks - C_LAG[0] + 1, kept(sent_c))

        @pl.when(t == settle)
        def _():
            own_c(c).wait_send()
            for i in range(3):
                weight_c(i, c).wait_send()
            own_up(lambda copy: copy.wait_send())
            own_down(lambda copy: copy.wait_send())
            own_full(lambda copy: copy.wait_send())


        whole_due = (t == GLOBAL_STEPS[0]) | (t == GLOBAL_STEPS[1]) | (t == GLOBAL_STEPS[2])

        @pl.when((s == OWNER) & whole_due)
        def _():
            src = jnp.where(t == GLOBAL_STEPS[0], OWNER, jnp.where(t == GLOBAL_STEPS[1], OWNER + 1, 0))
            global_step(src, 0, blocks, range(heads))

        @pl.when((s == OWNER) & (t == GLOBAL_STEPS[3]))
        def _():
            global_step(shards - 1, 2, blocks // 2, range(heads))

        return carry

    lax.fori_loop(0, span_main + c_lag, step, 0)

    @pl.when(s == OWNER)
    def _():
        for part in range(2):
            some = range(part * heads // 2, (part + 1) * heads // 2)
            global_step(shards - 1, 0, 2, some)
            global_step(shards - 1, blocks - 2, 2, some)
            for h in some:
                g_out[h] = (g_acc[h] / g_sum[h]).astype(jnp.bfloat16)
                result(h).start()

    for copy in tables:
        copy.wait()
    col = lax.broadcasted_iota(jnp.int32, (1, (5 + R) * B), 1)

    def columns(h):
        return pl.ds(pl.multiple_of(h * HD, HD), HD)

    def written(h, lead):
        part = pl.ds(0, DEPTH) if lead else pl.ds(DEPTH, rows - DEPTH)
        return pltpu.make_async_copy(o_ref.at[h, part], out_ref.at[part, columns(h)], osem.at[1 if lead else 0, h])

    def lead_rows(h):
        return pltpu.make_async_copy(g_in.at[h], out_ref.at[pl.ds(0, DEPTH), columns(h)], osem.at[1, h])

    def attend(h, carry):
        picks = []
        for j in range(blocks):
            g = s * blocks + j
            chosen = [jnp.clip(g + d, 0, total - 1) for d in (-1, 0, 1)] + [0, 1]
            for r in range(R):
                chosen.append(jnp.bitwise_xor(s, mask_ref[r]) * blocks + table_ref[r, h, g])
            picks.append(chosen)
        for j in range(blocks):
            keys = jnp.concatenate([k_s[h, p] for p in picks[j]], axis=0)
            scores_s[j] = lax.dot_general(q_s[h, j], keys, CONTRACT, preferred_element_type=jnp.float32)
        for j in range(blocks):
            place = s * blocks + j - 1 + col // B
            bias = jnp.where((col >= 3 * B) | ((place >= 2) & (place < total)), 0.0, -jnp.inf)
            scores = scores_s[j] * scale + bias
            expd = jnp.exp(scores - jnp.max(scores, axis=-1, keepdims=True))
            sum_s[j] = jnp.broadcast_to(jnp.sum(expd, axis=-1, keepdims=True), (B, HD))
            weight_s[j] = expd.astype(jnp.bfloat16)
        for j in range(blocks):
            values = jnp.concatenate([v_s[h, p] for p in picks[j]], axis=0)
            out = jnp.dot(weight_s[j], values, preferred_element_type=jnp.float32)
            o_ref[h, j * B:(j + 1) * B, :] = (out / sum_s[j]).astype(jnp.bfloat16)
        written(h, False).start()

        @pl.when(s != OWNER - 1)
        def _():
            written(h, True).start()

        return carry

    lax.fori_loop(0, heads, attend, 0)

    @pl.when(s == OWNER - 1)
    def _():
        for h in range(heads):
            result(h).wait_recv()
            lead_rows(h).start()
        for h in range(heads):
            lead_rows(h).wait()

    @pl.when(s == OWNER)
    def _():
        for h in range(heads):
            result(h).wait_send()

    @pl.when(s != OWNER - 1)
    def _():
        for h in range(heads):
            written(h, True).wait()

    for h in range(heads):
        written(h, False).wait()

    lax.fori_loop(span_main - DRAIN_LAG, span_main, lambda t, carry: (main(t, sent_main), carry)[1], 0)


def gathered_body(shards, tokens, projection, rand_table, round_masks):
    rows, width = tokens.shape
    mine = projection.shape[2] // 2
    heads = mine // HD
    blocks = rows // B
    dma = pltpu.SemaphoreType.DMA
    bf16, f32 = jnp.bfloat16, jnp.float32
    hbm = pl.BlockSpec(memory_space=pltpu.HBM)
    return pl.pallas_call(
        functools.partial(layer_kernel, shards),
        out_shape=jax.ShapeDtypeStruct((rows, mine), bf16),
        in_specs=[hbm, hbm, hbm, hbm],
        out_specs=hbm,
        scratch_shapes=[
            pltpu.VMEM((heads, rows, HD), bf16),
            pltpu.VMEM((shards, rows, 2 * width), bf16),
            pltpu.VMEM((3, 2 * width, mine), bf16),
            pltpu.VMEM((heads, blocks, B, HD), bf16),
            pltpu.VMEM((heads, shards * blocks, B, HD), bf16),
            pltpu.VMEM((heads, shards * blocks, B, HD), bf16),
            pltpu.VMEM((heads, 2, B, HD), bf16),
            pltpu.VMEM((heads, DEPTH, HD), f32),
            pltpu.VMEM((heads, DEPTH, HD), f32),
            pltpu.VMEM((heads, DEPTH, HD), f32),
            pltpu.VMEM((heads, DEPTH, HD), bf16),
            pltpu.VMEM((heads, DEPTH, HD), bf16),
            pltpu.VMEM((heads, DEPTH, rows), f32),
            pltpu.VMEM((heads, 2 * DEPTH, rows), bf16),
            pltpu.VMEM((blocks, B, (5 + R) * B), f32),
            pltpu.VMEM((blocks, B, (5 + R) * B), bf16),
            pltpu.VMEM((blocks, B, HD), f32),
            pltpu.SMEM((R, heads, shards * blocks), jnp.int32),
            pltpu.SMEM((R,), jnp.int32),
            dma((2, shards, blocks)),
            dma((shards, blocks)),
            dma((blocks,)),
            dma((blocks,)),
            dma((shards, blocks)),
            dma((shards, blocks)),
            dma((shards, blocks)),
            dma((shards, blocks)),
            dma((4,)),
            dma((4,)),
            dma((4,)),
            dma((2, heads)),
            dma((2,)),
            dma((2, heads)),
        ],
        compiler_params=pltpu.CompilerParams(
            collective_id=0, has_side_effects=True, vmem_limit_bytes=60 * 1024 * 1024
        ),
        name="layer",
    )(jnp.transpose(rand_table, (2, 0, 1)), round_masks, tokens, jnp.transpose(projection, (1, 0, 2)))


def solution(mesh):
    shards = mesh.shape["seq"]
    few = shards == R + 1 and mesh.shape["head"] == 2
    return jax.shard_map(
        functools.partial(gathered_body, shards) if few else body,
        mesh=mesh,
        in_specs=(
            P(("grp", "seq"), "rep"),
            P("rep", None, "head"),
            P(("head", "rep"), None, None),
            P(),
        ),
        out_specs=P(("grp", "seq"), ("head", "rep")),
        check_vma=False,
    )
```
